32 devices in a mesh: groups: 2 (over y), rows: 4 (over z), segment: 2 (over x), chan: 2 (over core).
Axes of the slice: x: 2, y: 2, z: 4, core: 2. Of those that a mesh axis runs over, the one named last changes fastest.
Arguments:
- latent: bfloat16 [8, 8, 160, 384], P(('groups', 'segment'), 'rows'), parts along dimension 0, may hold values from -6 to 6
- cache_mid: bfloat16 [4, 8, 160, 384], P('groups', 'rows'), parts along dimension 0, may hold values from -6 to 6
- cache_low: bfloat16 [4, 16, 320, 192], P('groups', 'rows'), parts along dimension 0, may hold values from -6 to 6
- gain_mid: float32 [384], replicated, may hold values from 0.1 to 1.9
- gain_attn: float32 [384], replicated, may hold values from 0.1 to 1.9
- gain_low: float32 [192], replicated, may hold values from 0.1 to 1.9
- conv_mid: bfloat16 [3, 3, 3, 384, 384], P(None, None, None, None, 'chan'), may hold values from -0.0625 to 0.0625
- attn_qkv: bfloat16 [384, 1152], replicated, may hold values from -4 to 4
- attn_proj: bfloat16 [384, 384], replicated, may hold values from -0.3125 to 0.3125
- conv_up: bfloat16 [3, 3, 384, 192], P(None, None, None, 'chan'), may hold values from -0.109375 to 0.109375
- conv_low: bfloat16 [3, 3, 3, 192, 192], P(None, None, None, None, 'chan'), may hold values from -0.078125 to 0.078125
Outputs:
- decoded: bfloat16 [8, 16, 320, 192], P(('groups', 'segment'), 'rows', None, 'chan'), parts along dimension 0
The draws below stay inside these ranges and needn't reach their ends.
There are 2 independent parts, one for each index of `groups`. The reference program is written for one: setup_inputs(seed, part) draws one part's arguments, and reference() takes and returns one part's arrays. A program takes and returns all parts, laid end to end along the dimension named above; an argument that names none is the same for every part. Nothing has to cross between parts.
All inputs are finite; a program needn't handle non-finite values.
Results may differ from the reference program's by a relative error of at most 0.0071.
Values may be sent and summed in bfloat16 or wider, within the bound.
A program may use at most 128 MiB of HBM per device.

```python
import math
import jax
import jax.numpy as jnp
from jax import lax

C1 = 384
C2 = 192
W = 160
H = 8
F = 4


def draw_attn_qkv(key, part):
    first_key = jax.random.fold_in(jax.random.fold_in(key, 17), 0)
    base = jax.random.normal(first_key, (C1, 3 * C1), jnp.float32) / math.sqrt(C1)
    return base.astype(jnp.bfloat16)


def block_scale(key, dims, pieces, smallest, high):
    factor_of, own = 1.0, jax.random.fold_in(key, 6)
    for axis_at, shards_of in pieces:
        steps = jnp.exp(jax.random.uniform(jax.random.fold_in(own, axis_at), (shards_of,), jnp.float32, smallest / len(pieces), high / len(pieces)))
        factor_of = factor_of * jnp.repeat(steps, dims[axis_at] // shards_of).reshape([-1 if axis == axis_at else 1 for axis in range(len(dims))])
    return factor_of


def noise(stream_key, shape, scale, bound, cuts=(), dtype=jnp.bfloat16):
    entries = jax.random.normal(stream_key, shape, jnp.float32) * scale
    if len(cuts) > 0:
        entries = block_scale(stream_key, shape, cuts, -0.22, 0.18) * entries
    return jnp.clip(entries, min=-bound, max=bound).astype(dtype)


def setup_inputs(seed: int = 0, part: int = 0) -> dict:
    seeds = jax.random.split(jax.random.key(seed), 12)
    part_keys = jax.random.split(jax.random.fold_in(seeds[11], part), 12)
    latent = noise(part_keys[0], (F, H, W, C1), 1.0, 6.0, ((0, 2), (1, 4)))
    cache_mid = noise(part_keys[1], (2, H, W, C1), 1.0, 6.0, ((1, 4),))
    cache_low = noise(part_keys[2], (2, 2 * H, 2 * W, C2), 1.0, 6.0, ((1, 4),))
    gain_mid = jnp.clip(1.0 + 0.18 * jax.random.normal(seeds[3], (C1,), jnp.float32), 0.1, 1.9)
    gain_attn = jnp.clip(1.0 + 0.18 * jax.random.normal(seeds[4], (C1,), jnp.float32), 0.1, 1.9)
    gain_low = jnp.clip(1.0 + 0.18 * jax.random.normal(seeds[5], (C2,), jnp.float32), 0.1, 1.9)
    conv_mid = noise(seeds[6], (3, 3, 3, C1, C1), (27 * C1) ** -0.5, 0.0625, ((4, 2),))
    attn_qkv = draw_attn_qkv(jax.random.fold_in(seeds[11], 71), part)
    attn_proj = noise(seeds[8], (C1, C1), C1 ** -0.5, 0.3125)
    conv_up = noise(seeds[9], (3, 3, C1, C2), (9 * C1) ** -0.5, 0.109375, ((3, 2),))
    conv_low = noise(seeds[10], (3, 3, 3, C2, C2), (27 * C2) ** -0.5, 0.078125, ((4, 2),))
    return dict(latent=latent, cache_mid=cache_mid, cache_low=cache_low, gain_mid=gain_mid, gain_attn=gain_attn, gain_low=gain_low, conv_mid=conv_mid, attn_qkv=attn_qkv, attn_proj=attn_proj, conv_up=conv_up, conv_low=conv_low)


def rms_scaled(values, scales):
    floated = values.astype(jnp.float32)
    return floated * lax.rsqrt(lax.optimization_barrier(jnp.mean(floated * floated, axis=-1, keepdims=True)) + 1e-06) * scales.astype(jnp.float32)

def causal_conv(sequence, kernel):
    return lax.conv_general_dilated(sequence[None].astype(jnp.float32), kernel.astype(jnp.float32), (1, 1, 1), ((0, 0), (1, 1), (1, 1)), dimension_numbers=('NDHWC', 'DHWIO', 'NDHWC'), precision=lax.Precision.HIGHEST)[0]

def reference(latent, cache_mid, cache_low, gain_mid, gain_attn, gain_low, conv_mid, attn_qkv, attn_proj, conv_up, conv_low):
    mid_in = jax.nn.silu(rms_scaled(latent, gain_mid)).astype(jnp.bfloat16)
    mid_seq = jnp.concatenate([cache_mid, mid_in], axis=0)
    segment_one = (latent.astype(jnp.float32) + causal_conv(mid_seq, conv_mid)).astype(jnp.bfloat16)
    attn_in = rms_scaled(segment_one, gain_attn).astype(jnp.bfloat16).reshape(F, H * W, C1)

    def one_frame(frame):
        qkv = jnp.dot(frame, attn_qkv, preferred_element_type=jnp.float32).astype(jnp.bfloat16)
        query = qkv[:, :C1]
        keys = qkv[:, C1:2 * C1]
        vals = qkv[:, 2 * C1:]
        scores = jnp.dot(query, keys.T, preferred_element_type=jnp.float32) / math.sqrt(C1)
        weights = jax.nn.softmax(scores, axis=-1).astype(jnp.bfloat16)
        mixed = jnp.dot(weights, vals, preferred_element_type=jnp.float32).astype(jnp.bfloat16)
        return jnp.dot(mixed, attn_proj, preferred_element_type=jnp.float32)
    branch = lax.map(one_frame, attn_in).reshape(F, H, W, C1)
    segment_two = (segment_one.astype(jnp.float32) + branch).astype(jnp.bfloat16)
    doubled = jnp.repeat(jnp.repeat(segment_two, 2, axis=1), 2, axis=2)
    upper = lax.conv_general_dilated(doubled.astype(jnp.float32), conv_up.astype(jnp.float32), (1, 1), ((1, 1), (1, 1)), dimension_numbers=('NHWC', 'HWIO', 'NHWC'), precision=lax.Precision.HIGHEST).astype(jnp.bfloat16)
    low_in = jax.nn.silu(rms_scaled(upper, gain_low)).astype(jnp.bfloat16)
    low_seq = jnp.concatenate([cache_low, low_in], axis=0)
    return (upper.astype(jnp.float32) + causal_conv(low_seq, conv_low)).astype(jnp.bfloat16)
```

```python
import functools
import math

import jax
import jax.numpy as jnp
from jax import lax
from jax.experimental import pallas as pl
from jax.experimental.pallas import tpu as pltpu
from jax.sharding import PartitionSpec as P

MESH = pl.DeviceIdType.MESH
BF = jnp.bfloat16
F32 = jnp.float32


class Place:
    def __init__(self):
        self.rows, self.segs = lax.axis_size("rows"), lax.axis_size("segment")
        self.z, self.s, self.c = (lax.axis_index(a) for a in ("rows", "segment", "chan"))
        self.up, self.down = self.z > 0, self.z < self.rows - 1
        self.has_next, self.has_prev = self.s < self.segs - 1, self.s > 0

    def greet(self):
        barrier = pltpu.get_barrier_semaphore()
        n = jnp.int32(1)
        pl.semaphore_signal(barrier, inc=1, device_id={"chan": 1 - self.c}, device_id_type=MESH)
        for ok, target in (
            (self.up, {"rows": self.z - 1}),
            (self.down, {"rows": self.z + 1}),
            (self.has_next, {"segment": self.s + 1}),
            (self.has_prev, {"segment": self.s - 1}),
        ):

            @pl.when(ok)
            def _():
                pl.semaphore_signal(barrier, inc=1, device_id=target, device_id_type=MESH)

            n = n + ok.astype(jnp.int32)
        pl.semaphore_wait(barrier, n)


def remote(src, dst, send, recv, target):
    return pltpu.make_async_remote_copy(
        src_ref=src, dst_ref=dst, send_sem=send, recv_sem=recv, device_id=target, device_id_type=MESH
    )


def normed(v, gain):
    return v * lax.rsqrt(jnp.mean(v * v, axis=-1, keepdims=True) + 1e-06) * gain


def silu(v):
    return 0.5 * v * (1.0 + jnp.tanh(0.5 * v))


def dot(a, b):
    return jnp.dot(a, b, preferred_element_type=F32)


def dot_t(a, b):
    return lax.dot_general(a, b, (((1,), (1,)), ((), ())), preferred_element_type=F32)


def run_taps(tap, taps_t, taps_h, frames, own):
    for back in range(taps_t):
        split = min(back, frames)
        low, high = (split, frames) if own else (0, split)
        if low < high:
            lax.fori_loop(0, taps_h, lambda i, _: (tap(taps_t - 1 - back, i, low, high), 0)[1], 0)


def picker(rows, cols, hit):
    k = lax.broadcasted_iota(jnp.int32, (rows, cols), 0)
    n = lax.broadcasted_iota(jnp.int32, (rows, cols), 1)
    return jnp.where(hit(k, n), 1.0, 0.0).astype(BF)


def first_part(
    here, latent_hbm, cache_hbm, gain_mid, w_hbm, every, begun, later,
    latent, xa, w, acc, edge_out, edge_in, seg, got, es, er, xs, xr, ps, pr, gs, gr, ls, wsem,
):
    frames, rows, width, ch = latent.shape
    taps_t, taps_h, taps_w, part = w.shape[:4]
    before = taps_t - 1
    c, z = here.c, here.z
    first = jnp.logical_not(here.has_prev)
    order = (2, 0, 1)
    own = pltpu.make_async_copy(latent_hbm, latent, ls.at[0])
    local = pltpu.make_async_copy(cache_hbm, xa.at[pl.ds(0, before)], ls.at[1])
    weights = [pltpu.make_async_copy(w_hbm.at[:, kh], w.at[:, kh], wsem.at[kh]) for kh in order]
    own.start()
    pl.when(first)(lambda: local.start())
    for fetch in weights:
        fetch.start()
    acc[...] = jnp.zeros(acc.shape, F32)
    here.greet()
    begun()

    across = remote(xa.at[before + c], xa.at[c], xs, xr, {"segment": here.s + 1})
    share = remote(xa.at[c], xa.at[c], ps, pr, {"chan": 1 - c})
    to_up = remote(edge_out.at[0], edge_in.at[1], es.at[0], er.at[1], {"rows": z - 1})
    to_down = remote(edge_out.at[1], edge_in.at[0], es.at[1], er.at[0], {"rows": z + 1})
    swap = remote(seg.at[1 - c], got, gs, gr, {"chan": 1 - c})

    own.wait()
    gain = gain_mid[...].reshape(1, ch)

    def fill(f):
        for r in range(rows):
            xa[before + f, r] = silu(normed(latent[f, r].astype(F32), gain)).astype(BF)

    fill(c)
    pl.when(here.has_next)(lambda: across.start())
    fill(1 - c)
    pick = picker(ch, part, lambda k, n: k == n + c * part)
    for t in range(frames):
        acc[1, t, 1 : 1 + rows] = dot(latent[t].reshape(rows * width, ch), pick).reshape(rows, width, part)

    def taps(kh, mine):
        def each(kw, _):
            for t in range(frames):
                some = [kt for kt in range(taps_t) if (t + kt >= before) == mine]
                if some:
                    left = jnp.concatenate([xa[t + kt].reshape(rows * width, ch) for kt in some], axis=1)
                    right = jnp.concatenate([w[kt, kh, kw] for kt in some], axis=1)
                    acc[kw, t, 2 - kh : 2 - kh + rows] += dot_t(left, right).reshape(rows, width, part)
            return 0

        lax.fori_loop(0, taps_w, each, 0)

    for fetch, kh in zip(weights, order[:2]):
        fetch.wait()
        taps(kh, True)
    weights[2].wait()

    @pl.when(here.has_prev)
    def _():
        taps(1, True)
        across.wait_recv()
        share.start()
        share.wait_recv()

    pl.when(first)(lambda: local.wait())
    for kh in order[:2]:
        taps(kh, False)
    col = lax.broadcasted_iota(jnp.int32, (width, part), 0)

    def joined(t, row):
        left = jnp.where(col == 0, 0.0, pltpu.roll(acc[0, t, row], 1, 0))
        right = jnp.where(col == width - 1, 0.0, pltpu.roll(acc[2, t, row], width - 1, 0))
        return acc[1, t, row] + left + right

    for k, row in enumerate((0, rows + 1)):
        for t in range(frames):
            edge_out[k, t] = joined(t, row).astype(BF)
    pl.when(here.up)(lambda: to_up.start())
    pl.when(here.down)(lambda: to_down.start())
    pl.when(first)(lambda: taps(1, True))
    taps(1, False)
    later()
    for ok, copy, k, row in ((here.up, to_down, 0, 1), (here.down, to_up, 1, rows)):

        @pl.when(ok)
        def _():
            copy.wait_recv()
            for t in range(frames):
                acc[1, t, row] += edge_in[k, t].astype(F32)

    def finish(t):
        for r in range(rows):
            seg[t, r] = joined(t, 1 + r).astype(BF)

    finish(1 - c)
    swap.start()
    finish(c)
    put = [picker(part, ch, lambda k, n: n == k + off * part) for off in (c, 1 - c)]
    full = dot(seg[c].reshape(rows * width, part), put[0])
    swap.wait_recv()
    full = full + dot(got[...].reshape(rows * width, part), put[1])
    full = full.astype(BF).reshape(rows, width, ch)
    for r in range(rows):
        every[z * rows + r] = full[r]

    def drain():
        swap.wait_send()
        pl.when(here.has_prev)(lambda: share.wait_send())
        pl.when(here.has_next)(lambda: across.wait_send())
        pl.when(here.up)(lambda: to_up.wait_send())
        pl.when(here.down)(lambda: to_down.wait_send())

    return drain


def attn_part(
    here, later, gain_attn, wqk, wvo, every, own, across,
    keys, q_own, q_edge, y_own, y_edge, top_own, top_edge, sum_own, sum_edge, send, recv,
):
    total, width, ch = every.shape
    z, chips = here.z, here.rows
    rows = total // chips
    mine = z * rows
    gain = gain_attn[...].reshape(1, ch)
    sides = ((-1, here.down, {"rows": z + 1}), (1, here.up, {"rows": z - 1}))

    def copy(row, side):
        return remote(every.at[row], every.at[row], send.at[row, side], recv.at[row], sides[side][2])

    def turn(side, r):
        return r if side else rows - 1 - r

    for r in range(rows):
        for side, (_, ok, _) in enumerate(sides):
            pl.when(ok)(lambda: copy(mine + turn(side, r), side).start())

    def norm_rows(src):
        for r in range(rows):
            keys[src * rows + r] = normed(every[src * rows + r].astype(F32), gain).astype(BF)

    def update(chunk, src):
        q, y, top, total = chunk
        some = keys[pl.ds(src * rows, rows)].reshape(rows * width, ch)
        s = dot_t(q[...], some)
        high = jnp.maximum(top[...], jnp.max(s, axis=-1, keepdims=True))
        p = jnp.exp2(s - high)
        fade = jnp.exp2(top[...] - high)
        top[...] = high
        total[...] = total[...] * fade + jnp.sum(p, axis=-1, keepdims=True)
        y[...] = y[...] * fade + dot(p.astype(BF), some)

    inner = (q_own, y_own, top_own, sum_own)
    outer = (q_edge, y_edge, top_edge, sum_edge)
    for _, y, top, count in (inner, outer):
        y[...] = jnp.zeros(y.shape, F32)
        top[...] = jnp.full(top.shape, -jnp.inf, F32)
        count[...] = jnp.zeros(count.shape, F32)
    norm_rows(z)
    q_own[...] = dot(keys[pl.ds(mine, rows)].reshape(rows * width, ch), wqk[...]).astype(BF)
    update(inner, z)
    later()
    edges = ((here.up, mine - 1, 0), (here.down, mine + rows, 1))

    def spots(k):
        return ((z - k, z - k >= 0), (z + k, z + k < chips))

    def outer_update(k):
        for src, valid in spots(k):
            pl.when(valid)(lambda: update(outer, src))

    def hop(k, _):
        for side, (src, valid) in enumerate(spots(k)):

            @pl.when(valid)
            def _():
                for r in range(rows):
                    row = src * rows + turn(side, r)
                    copy(row, side).wait_recv()
                    pl.when(sides[side][1])(lambda: copy(row, side).start())
                norm_rows(src)
                update(inner, src)

        @pl.when(k == 1)
        def _():
            for ok, row, at in edges:
                part = pl.ds(at * width, width)

                @pl.when(ok)
                def _():
                    q_edge[part, :] = dot(keys[row], wqk[...]).astype(BF)

                @pl.when(jnp.logical_not(ok))
                def _():
                    q_edge[part, :] = jnp.zeros((width, ch), BF)

            update(outer, z)

        pl.when(k > 1)(lambda: outer_update(k - 1))
        return 0

    lax.fori_loop(1, chips, hop, 0)

    def close(chunk):
        _, y, _, count = chunk
        return dot((y[...] / count[...]).astype(BF), wvo[...])

    o = close(inner)
    for r in range(rows):
        own[1 + r] = (every[mine + r].astype(F32) + o[r * width : (r + 1) * width]).astype(BF)
        pl.when(here.has_next)(lambda: across[r].start())
    outer_update(chips - 1)
    o = close(outer)
    for ok, row, at in edges:
        slot = at * (rows + 1)

        @pl.when(ok)
        def _():
            own[slot] = (every[row].astype(F32) + o[at * width : (at + 1) * width]).astype(BF)

        @pl.when(jnp.logical_not(ok))
        def _():
            own[slot] = jnp.zeros((width, ch), BF)

    def drain():
        def each(k, _):
            for side, (src, valid) in enumerate(spots(k)):

                @pl.when(valid & sides[side][1])
                def _():
                    for r in range(rows):
                        copy(src * rows + r, side).wait_send()

            return 0

        lax.fori_loop(0, chips, each, 0)

    return drain


def last_part(
    here, own, cache, gain, wup, wlow_hbm, out, across,
    x, acc, wlow, prior, chalo, wfull, wmix, wtap, grid, upper,
    ps, pr, cs, cr, ws, wr, ls, fs, es, er, us, ur,
):
    frames = cache.shape[0]
    height, width, ch = own.shape
    c, z = here.c, here.z
    tall = cache.shape[1]
    low = cache.shape[2]
    wide = cache.shape[3]
    two = 2 * low
    part = wup.shape[2]
    first = jnp.logical_not(here.has_prev)
    fetch = pltpu.make_async_copy(wlow_hbm, wlow, fs)
    fetch.start()
    local = pltpu.make_async_copy(wup, wfull.at[c], ls)
    local.start()
    relays = (
        (0, here.up, remote(prior.at[1], prior.at[height - 1], ps.at[0], pr.at[0], {"rows": z - 1})),
        (height - 3, here.down, remote(prior.at[height - 2], prior.at[0], ps.at[1], pr.at[1], {"rows": z + 1})),
    )
    to_up = remote(cache.at[:, 0], chalo.at[1], cs.at[0], cr.at[0], {"rows": z - 1})
    to_down = remote(cache.at[:, tall - 1], chalo.at[0], cs.at[1], cr.at[1], {"rows": z + 1})
    weights = remote(wup, wfull.at[c], ws, wr, {"chan": 1 - c})

    weights.start()
    yield
    for edge, inside in ((0, here.up), (own.shape[0] - 1, here.down)):

        @pl.when(jnp.logical_not(inside))
        def _():
            prior[edge] = jnp.zeros(own.shape[1:], BF)

    taps_t, taps_h = wlow.shape[:2]
    fetch.wait()

    def lay(i, _):
        kt, kh = i // taps_h, i % taps_h
        tap = [wlow[kt, kh, k * low : (k + 1) * low] for k in range(3)]
        none = jnp.zeros((low, part), BF)
        blocks = ((tap[1], tap[0]), (tap[2], tap[1]), (none, tap[2]), (tap[0], none))
        for at, (even, odd) in enumerate(blocks):
            wtap[kt, kh, at * low : (at + 1) * low, :] = jnp.concatenate([even, odd], axis=1)
        return 0

    lax.fori_loop(0, taps_t * taps_h, lay, 0)

    local.wait()
    weights.wait_recv()
    for kh in range(3):
        for at, sides in enumerate(((1, 1), (2, 0), (0, 2))):
            for side, kw in enumerate(sides):
                for half in (0, 1):
                    start = side * low + half * part
                    wmix[kh, at, start : start + part] = wfull[half, kh, kw]

    yield
    pl.when(first & here.up)(lambda: to_up.start())
    pl.when(first & here.down)(lambda: to_down.start())

    gains = gain[...].reshape(1, low)
    gains = jnp.concatenate([gains, gains], axis=1)
    lane = lax.broadcasted_iota(jnp.int32, (width, two), 1)
    col = lax.broadcasted_iota(jnp.int32, (width, two), 0)
    evens = lane < low

    def spaced(v, keep_first, keep_last):
        v_next = jnp.where(col == width - 1, 0.0, pltpu.roll(v, width - 1, 0))
        v_prev = jnp.where(col == 0, 0.0, pltpu.roll(v, 1, 0))
        return jnp.where(evens, keep_first(v_prev, v_next), keep_last(v_prev, v_next))

    def beside(slot, row, v):
        x[slot, tall + 2 + row] = spaced(v, lambda p, n: n, lambda p, n: p).astype(BF)

    def put(slot, row, v):
        x[slot, row] = v.astype(BF)
        beside(slot, row, v)

    def row_copy(slot, at, r):
        piece = x.at[slot, r]
        return remote(piece, piece, es.at[at, r], er.at[at, r], {"chan": 1 - c})

    def upper_copy(f, r):
        return remote(upper.at[f, r], upper.at[f, r], us.at[r], ur.at[r], {"chan": 1 - c})

    def raise_frame(tile, at):
        slot = at * frames + c
        for kh in range(3):
            n0, n1 = (0, height - 1) if kh == 0 else (0, height) if kh == 1 else (1, height)
            flat = tile[n0:n1].reshape((n1 - n0) * width, ch)
            g0 = sum((height - 1, height)[:kh])
            g1 = g0 + n1 - n0
            grid[g0:g1, :, :two] = (dot_t(flat, wmix[kh, 0]) + dot_t(flat, wmix[kh, 1])).reshape(
                n1 - n0, width, two
            )
            grid[g0:g1, :, two:] = dot_t(flat, wmix[kh, 2]).reshape(n1 - n0, width, two)
        for r in range(tall + 2):
            i, odd = (r + 1) // 2, (r + 1) % 2
            sources = (i, i, i + 1) if odd else (i - 1, i, i)
            both = grid[sources[0]] + grid[height - 1 + sources[1]] + grid[2 * height - 2 + sources[2]]
            v = both[:, :two] + spaced(both[:, two:], lambda p, n: p, lambda p, n: n)
            v = v.astype(BF)
            if at and 0 < r <= tall:
                upper[c, r - 1] = v
                upper_copy(c, r - 1).start()
            v = v.astype(F32)
            sq = v * v
            mean_even = jnp.sum(jnp.where(evens, sq, 0.0), axis=-1, keepdims=True) / low
            mean_odd = jnp.sum(jnp.where(evens, 0.0, sq), axis=-1, keepdims=True) / low
            v = v * jnp.where(evens, lax.rsqrt(mean_even + 1e-06), lax.rsqrt(mean_odd + 1e-06)) * gains
            v = silu(v)
            if r == 0:
                v = jnp.where(here.up, v, 0.0)
            if r == tall + 1:
                v = jnp.where(here.down, v, 0.0)
            put(slot, r, v)
            row_copy(slot, at, r).start()
        other = at * frames + 1 - c
        for r in range(tall + 2):
            row_copy(other, at, r).wait_recv()
            beside(other, r, x[other, r].astype(F32))

    raise_frame(own, 1)

    @pl.when(here.has_prev)
    def _():
        for r, copy in enumerate(across):
            copy.wait_recv()
            for at, ok, relay in relays:
                if at == r:
                    pl.when(ok)(lambda: relay.start())

    acc[...] = jnp.zeros(acc.shape, F32)

    def tap(kt, kh, low, high):
        def plane(k):
            at = pl.ds(k * (tall + 2) + kh, tall)
            return x[low + kt : high + kt, at].reshape((high - low) * tall * width, two)

        v = jnp.concatenate([plane(0), plane(1)], axis=1)
        acc[low * tall * width : high * tall * width] += dot(v, wtap[kt, kh])

    run_taps(tap, taps_t, taps_h, frames, True)

    @pl.when(here.has_prev)
    def _():
        pl.when(here.down)(lambda: relays[0][2].wait_recv())
        pl.when(here.up)(lambda: relays[1][2].wait_recv())
        raise_frame(prior, 0)

    spots = [picker(width, wide, lambda k, n: n == 2 * k + p) for p in (0, 1)]

    def take(slot, row, flipped):
        put(slot, row, jnp.concatenate([dot_t(spot, flipped) for spot in spots], axis=1))

    @pl.when(first)
    def _():
        def each(i, _):
            take(i // tall, 1 + i % tall, cache[i // tall, i % tall])
            return 0

        lax.fori_loop(0, frames * tall, each, 0)

    for row, inside, k, copy in ((0, here.up, 0, to_down), (tall + 1, here.down, 1, to_up)):

        @pl.when(first & inside)
        def _():
            copy.wait_recv()
            for f in range(frames):
                take(f, row, chalo[k, f])

        @pl.when(first & jnp.logical_not(inside))
        def _():
            for f in range(frames):
                put(f, row, jnp.zeros((width, two), F32))

    run_taps(tap, taps_t, taps_h, frames, False)
    n = 2 * part
    pick = picker(two, n, lambda k, j: k == jnp.where(j < part, j, j - part + low) + c * part)
    for r in range(tall):
        upper_copy(1 - c, r).wait_recv()
    acc[...] += dot(upper[...].reshape(-1, two), pick)

    def finish(i, _):
        done = acc[pl.ds(pl.multiple_of(i * width, width), width), :].T.astype(BF)
        out[i // tall, i % tall] = (dot(done[:part], spots[0]) + dot(done[part:], spots[1])).astype(BF)
        return 0

    lax.fori_loop(0, frames * tall, finish, 0)
    weights.wait_send()
    for r in range(tall):
        upper_copy(c, r).wait_send()
    for r in range(tall + 2):
        row_copy(frames + c, 1, r).wait_send()

    @pl.when(here.has_prev)
    def _():
        for _, ok, relay in relays:
            pl.when(ok)(lambda: relay.wait_send())
        for r in range(tall + 2):
            row_copy(c, 0, r).wait_send()

    for copy in across:
        pl.when(here.has_next)(lambda: copy.wait_send())
    pl.when(first & here.up)(lambda: to_up.wait_send())
    pl.when(first & here.down)(lambda: to_down.wait_send())


def whole_kernel(counts, *refs):
    groups = []
    for count in counts:
        groups.append(refs[:count])
        refs = refs[count:]
    ins, (out,), shared, first, attn, last = groups
    latent, cache_mid, cache_low, gain_mid, gain_attn, gain_low, conv_mid, attn_qkv, attn_proj, conv_up, conv_low = ins
    every, own, prior, wqkv, wproj, wqk, wvo, low_cache, sems, xs, xr = shared
    fetches = [
        pltpu.make_async_copy(src, dst, sems.at[i])
        for i, (src, dst) in enumerate(((attn_qkv, wqkv), (attn_proj, wproj), (cache_low, low_cache)))
    ]
    here = Place()
    rows, ch = own.shape[0] - 2, own.shape[2]
    across = [
        remote(own.at[1 + r], prior.at[1 + r], xs.at[r], xr.at[r], {"segment": here.s + 1}) for r in range(rows)
    ]
    tail = last_part(here, own, low_cache, gain_low, conv_up, conv_low, out, across, *last[:2], last[2], prior, *last[3:])

    def begun():
        for fetch in fetches:
            fetch.start()
        next(tail)

    def fold():
        for fetch in fetches:
            fetch.wait()
        wqk[...] = (dot_t(wqkv[:, :ch], wqkv[:, ch : 2 * ch]) * (math.log2(math.e) / math.sqrt(ch))).astype(BF)
        wvo[...] = dot(wqkv[:, 2 * ch :], wproj[...]).astype(BF)

    drains = [first_part(here, latent, cache_mid, gain_mid, conv_mid, every, begun, fold, *first)]
    drains.append(attn_part(here, lambda: next(tail), gain_attn, wqk, wvo, every, own, across, *attn))
    next(tail, None)
    for drain in drains:
        drain()


def call(kernel, number, outs, scratch, *args, far=()):
    return pl.pallas_call(
        kernel,
        out_shape=outs,
        in_specs=[pl.BlockSpec(memory_space=pl.ANY if i in far else pltpu.VMEM) for i in range(len(args))],
        out_specs=jax.tree.map(lambda _: pl.BlockSpec(memory_space=pltpu.VMEM), outs),
        scratch_shapes=scratch,
        compiler_params=pltpu.CompilerParams(
            collective_id=number, has_side_effects=True, vmem_limit_bytes=67043328
        ),
    )(*args)


def body(
    latent, cache_mid, cache_low, gain_mid, gain_attn, gain_low, conv_mid, attn_qkv, attn_proj, conv_up, conv_low
):
    frames, rows, width, ch = latent.shape
    part = conv_mid.shape[-1]
    dma, one = pltpu.SemaphoreType.DMA, pltpu.SemaphoreType.DMA(())
    taps_t, taps_h, taps_w = conv_mid.shape[:3]
    total = rows * lax.axis_size("rows")
    cache_t = jnp.swapaxes(cache_low, 2, 3)
    tile = pltpu.VMEM((rows + 2, width, ch), BF)
    shared = [
        pltpu.VMEM((total, width, ch), BF), tile, tile,
        pltpu.VMEM(attn_qkv.shape, BF), pltpu.VMEM(attn_proj.shape, BF),
        pltpu.VMEM((ch, ch), BF), pltpu.VMEM((ch, ch), BF), pltpu.VMEM(cache_t.shape, BF),
        dma((3,)), dma((rows,)), dma((rows,)),
    ]
    first = [
        pltpu.VMEM(latent.shape, BF),
        pltpu.VMEM((taps_t - 1 + frames, rows, width, ch), BF),
        pltpu.VMEM((taps_t, taps_h, taps_w, part, ch), BF),
        pltpu.VMEM((taps_w, frames, rows + 2, width, part), F32),
        pltpu.VMEM((2, frames, width, part), BF),
        pltpu.VMEM((2, frames, width, part), BF),
        pltpu.VMEM((frames, rows, width, part), BF),
        pltpu.VMEM((rows, width, part), BF),
        dma((2,)), dma((2,)), one, one, one, one, one, one, dma((2,)), dma((taps_h,)),
    ]
    sizes = (rows * width, 2 * width)
    attn = [
        pltpu.VMEM((total, width, ch), BF),
        *(pltpu.VMEM((n, ch), BF) for n in sizes),
        *(pltpu.VMEM((n, ch), F32) for n in sizes),
        *(pltpu.VMEM((n, 1), F32) for n in sizes),
        *(pltpu.VMEM((n, 1), F32) for n in sizes),
        dma((total, 2)),
        dma((total,)),
    ]
    _, tall, wide, low = cache_low.shape
    cut = conv_low.shape[-1]
    two = 2 * low
    taps_t, taps_h, taps_w = conv_low.shape[:3]
    last = [
        pltpu.VMEM((2 * frames, 2 * (tall + 2), width, two), BF),
        pltpu.VMEM((frames * tall * width, 2 * cut), F32),
        pltpu.VMEM((taps_t, taps_h, taps_w * low, cut), BF),
        pltpu.VMEM((2, frames, low, wide), BF),
        pltpu.VMEM((2, 3, 3, cut, ch), BF),
        pltpu.VMEM((3, 3, two, ch), BF),
        pltpu.VMEM((taps_t, taps_h, 2 * two, 2 * cut), BF),
        pltpu.VMEM((3 * rows + 4, width, 2 * two), F32),
        pltpu.VMEM((frames, tall, width, two), BF),
        dma((2,)), dma((2,)), dma((2,)), dma((2,)), one, one, one, one,
        dma((2, tall + 2)), dma((2, tall + 2)), dma((tall,)), dma((tall,)),
    ]
    args = (
        latent, cache_mid, cache_t, gain_mid, gain_attn, gain_low, jnp.swapaxes(conv_mid, 3, 4), attn_qkv, attn_proj,
        jnp.swapaxes(conv_up, 2, 3), conv_low.reshape(taps_t, taps_h, taps_w * low, cut),
    )
    counts = (len(args), 1, len(shared), len(first), len(attn), len(last))
    decoded = call(
        functools.partial(whole_kernel, counts),
        0,
        jax.ShapeDtypeStruct((frames, tall, cut, wide), BF),
        shared + first + attn + last,
        *args,
        far=(0, 1, 2, 6, 7, 8, 9, 10),
    )
    return jnp.swapaxes(decoded, 2, 3)


def solution(mesh):
    placed = (
        P(("groups", "segment"), "rows", None, None),
        P("groups", "rows", None, None),
        P("groups", "rows", None, None),
        P(),
        P(),
        P(),
        P(None, None, None, None, "chan"),
        P(),
        P(),
        P(None, None, None, "chan"),
        P(None, None, None, None, "chan"),
    )
    return jax.shard_map(
        body,
        mesh=mesh,
        in_specs=placed,
        out_specs=P(("groups", "segment"), "rows", None, "chan"),
        check_vma=False,
    )
```

```python
import functools
import math

import jax
import jax.numpy as jnp
from jax import lax
from jax.experimental import pallas as pl
from jax.experimental.pallas import tpu as pltpu
from jax.sharding import PartitionSpec as P

MESH = pl.DeviceIdType.MESH
BF = jnp.bfloat16
F32 = jnp.float32


class Place:
    def __init__(self):
        self.rows, self.segs = lax.axis_size("rows"), lax.axis_size("segment")
        self.z, self.s, self.c = (lax.axis_index(a) for a in ("rows", "segment", "chan"))
        self.up, self.down = self.z > 0, self.z < self.rows - 1
        self.has_next, self.has_prev = self.s < self.segs - 1, self.s > 0

    def greet(self):
        barrier = pltpu.get_barrier_semaphore()
        n = jnp.int32(1)
        pl.semaphore_signal(barrier, inc=1, device_id={"chan": 1 - self.c}, device_id_type=MESH)
        for ok, target in (
            (self.up, {"rows": self.z - 1}),
            (self.down, {"rows": self.z + 1}),
            (self.has_next, {"segment": self.s + 1}),
            (self.has_prev, {"segment": self.s - 1}),
        ):

            @pl.when(ok)
            def _():
                pl.semaphore_signal(barrier, inc=1, device_id=target, device_id_type=MESH)

            n = n + ok.astype(jnp.int32)
        return lambda: pl.semaphore_wait(barrier, n)


def remote(src, dst, send, recv, target):
    return pltpu.make_async_remote_copy(
        src_ref=src, dst_ref=dst, send_sem=send, recv_sem=recv, device_id=target, device_id_type=MESH
    )


def normed(v, gain):
    return v * lax.rsqrt(jnp.mean(v * v, axis=-1, keepdims=True) + 1e-06) * gain


def silu(v):
    return 0.5 * v * (1.0 + jnp.tanh(0.5 * v))


def dot(a, b):
    return jnp.dot(a, b, preferred_element_type=F32)


def dot_t(a, b):
    return lax.dot_general(a, b, (((1,), (1,)), ((), ())), preferred_element_type=F32)


def picker(rows, cols, hit):
    k = lax.broadcasted_iota(jnp.int32, (rows, cols), 0)
    n = lax.broadcasted_iota(jnp.int32, (rows, cols), 1)
    return jnp.where(hit(k, n), 1.0, 0.0).astype(BF)


def first_part(
    here, latent_hbm, cache_hbm, gain_mid, w_hbm, every, begun, later,
    latent, xa, w, acc, edge_out, edge_in, seg, got, es, er, xs, xr, ps, pr, gs, gr, ls, wsem,
):
    frames, rows, width, ch = latent.shape
    taps_t, taps_h, taps_w, part = w.shape[:4]
    before = taps_t - 1
    c, z = here.c, here.z
    first = jnp.logical_not(here.has_prev)
    order = (2, 0, 1)
    met = here.greet()
    own = pltpu.make_async_copy(latent_hbm, latent, ls.at[0])
    local = pltpu.make_async_copy(cache_hbm, xa.at[pl.ds(0, before)], ls.at[1])
    weights = [pltpu.make_async_copy(w_hbm.at[:, kh], w.at[:, kh], wsem.at[kh]) for kh in order]
    own.start()
    pl.when(first)(lambda: local.start())
    for fetch in weights:
        fetch.start()
    acc[...] = jnp.zeros(acc.shape, F32)
    half = rows // 2

    def piece(f):
        return xa.at[f, pl.ds(c * half, half)]

    across = [remote(piece(before + f), piece(f), xs.at[f], xr.at[f], {"segment": here.s + 1}) for f in range(before)]
    share = [remote(piece(f), piece(f), ps.at[f], pr.at[f], {"chan": 1 - c}) for f in range(before)]
    to_up = remote(edge_out.at[0], edge_in.at[1], es.at[0], er.at[1], {"rows": z - 1})
    to_down = remote(edge_out.at[1], edge_in.at[0], es.at[1], er.at[0], {"rows": z + 1})
    swap = remote(seg.at[1 - c], got, gs, gr, {"chan": 1 - c})

    own.wait()
    gain = gain_mid[...].reshape(1, ch)

    def fill(f, side):
        for r in range(half):
            row = side * half + r
            xa[before + f, row] = silu(normed(latent[f, row].astype(F32), gain)).astype(BF)

    late = tuple(range(before))[::-1]
    fill(late[0], c)
    met()
    for f in late:
        if f != late[0]:
            fill(f, c)
        pl.when(here.has_next)(lambda: across[f].start())
    begun()
    for f in range(frames):
        fill(f, 1 - c)
    pick = picker(ch, part, lambda k, n: k == n + c * part)
    for t in range(frames):
        acc[1, t, 1 : 1 + rows] = dot(latent[t].reshape(rows * width, ch), pick).reshape(rows, width, part)

    def taps(kh, *uses):
        def each(kw, _):
            for t, some in uses:
                left = jnp.concatenate([xa[t + kt].reshape(rows * width, ch) for kt in some], axis=1)
                right = jnp.concatenate([w[kt, kh, kw] for kt in some], axis=1)
                acc[kw, t, 2 - kh : 2 - kh + rows] += dot_t(left, right).reshape(rows, width, part)
            return 0

        lax.fori_loop(0, taps_w, each, 0)

    def uses(frames_in):
        return [(t, some) for t in range(frames) if (some := [kt for kt in range(taps_t) if t + kt in frames_in])]

    fresh = uses(range(before, before + frames))
    stale = uses(range(before))
    for fetch, kh in zip(weights, order[:2]):
        fetch.wait()
        taps(kh, *fresh)
    weights[2].wait()

    @pl.when(here.has_prev)
    def _():
        taps(order[2], *fresh)
        for f in late:
            across[f].wait_recv()
            share[f].start()
            share[f].wait_recv()
            for kh in order[:2]:
                taps(kh, *uses((f,)))

    @pl.when(first)
    def _():
        local.wait()
        for kh in order[:2]:
            taps(kh, *stale)

    col = lax.broadcasted_iota(jnp.int32, (width, part), 0)

    def joined(t, row):
        left = jnp.where(col == 0, 0.0, pltpu.roll(acc[0, t, row], 1, 0))
        right = jnp.where(col == width - 1, 0.0, pltpu.roll(acc[2, t, row], width - 1, 0))
        return acc[1, t, row] + left + right

    for k, row in enumerate((0, rows + 1)):
        edge_out[k] = jnp.concatenate([joined(t, row) for t in range(frames)], axis=1).astype(BF)
    pl.when(here.up)(lambda: to_up.start())
    pl.when(here.down)(lambda: to_down.start())
    pl.when(first)(lambda: taps(order[2], *fresh))
    taps(order[2], *stale)
    later()
    for ok, copy, k, row in ((here.up, to_down, 0, 1), (here.down, to_up, 1, rows)):

        @pl.when(ok)
        def _():
            copy.wait_recv()
            got_edge = edge_in[k].astype(F32)
            for t in range(frames):
                acc[1, t, row] += got_edge[:, t * part : (t + 1) * part]

    def finish(t):
        for r in range(rows):
            v = joined(t, 1 + r)
            seg[t, r] = jnp.concatenate([v, v], axis=1).astype(BF)

    finish(1 - c)
    swap.start()
    finish(c)
    lower = lax.broadcasted_iota(jnp.int32, (width, ch), 1) < part
    kept = lower == (c == 0)
    swap.wait_recv()
    for r in range(rows):
        every[z * rows + r] = jnp.where(kept, seg[c, r].astype(F32), got[r].astype(F32)).astype(BF)

    def drain():
        swap.wait_send()
        for f in late:
            pl.when(here.has_prev)(lambda: share[f].wait_send())
            pl.when(here.has_next)(lambda: across[f].wait_send())
        pl.when(here.up)(lambda: to_up.wait_send())
        pl.when(here.down)(lambda: to_down.wait_send())

    return drain


def attn_part(
    here, later, gain_attn, wqk, wvo, every, own, across,
    keys, q_own, q_edge, y_own, y_edge, top_own, top_edge, sum_own, sum_edge, send, recv,
):
    total, width, ch = every.shape
    z, chips = here.z, here.rows
    rows = total // chips
    mine = z * rows
    gain = gain_attn[...].reshape(1, ch)
    sides = ((-1, here.down, {"rows": z + 1}), (1, here.up, {"rows": z - 1}))

    def copy(row, side):
        return remote(every.at[row], every.at[row], send.at[row, side], recv.at[row], sides[side][2])

    def turn(side, r):
        return r if side else rows - 1 - r

    for r in range(rows):
        for side, (_, ok, _) in enumerate(sides):
            pl.when(ok)(lambda: copy(mine + turn(side, r), side).start())

    def norm_rows(src):
        for r in range(rows):
            keys[src * rows + r] = normed(every[src * rows + r].astype(F32), gain).astype(BF)

    def update(chunk, src):
        q, y, top, total = chunk
        some = keys[pl.ds(src * rows, rows)].reshape(rows * width, ch)
        s = dot_t(q[...], some)
        high = jnp.maximum(top[...], jnp.max(s, axis=-1, keepdims=True))
        p = jnp.exp2(s - high)
        fade = jnp.exp2(top[...] - high)
        top[...] = high
        total[...] = total[...] * fade + jnp.sum(p, axis=-1, keepdims=True)
        y[...] = y[...] * fade + dot(p.astype(BF), some)

    inner = (q_own, y_own, top_own, sum_own)
    outer = (q_edge, y_edge, top_edge, sum_edge)
    for _, y, top, count in (inner, outer):
        y[...] = jnp.zeros(y.shape, F32)
        top[...] = jnp.full(top.shape, -jnp.inf, F32)
        count[...] = jnp.zeros(count.shape, F32)
    norm_rows(z)
    q_own[...] = dot(keys[pl.ds(mine, rows)].reshape(rows * width, ch), wqk[...]).astype(BF)
    update(inner, z)
    later()
    edges = ((here.up, mine - 1, 0), (here.down, mine + rows, 1))

    def spots(k):
        return ((z - k, z - k >= 0), (z + k, z + k < chips))

    def outer_update(k):
        for src, valid in spots(k):
            pl.when(valid)(lambda: update(outer, src))

    def outer_start():
        for ok, row, at in edges:
            part = pl.ds(at * width, width)

            @pl.when(ok)
            def _():
                q_edge[part, :] = dot(keys[row], wqk[...]).astype(BF)

            @pl.when(jnp.logical_not(ok))
            def _():
                q_edge[part, :] = jnp.zeros((width, ch), BF)

        update(outer, z)

    def land(k, r):
        for side, (src, valid) in enumerate(spots(k)):

            @pl.when(valid)
            def _():
                row = src * rows + turn(side, r)
                copy(row, side).wait_recv()
                pl.when(sides[side][1])(lambda: copy(row, side).start())

    def hop(k, _):
        land(k, 0)
        pl.when(k == 2)(outer_start)
        pl.when(k > 1)(lambda: outer_update(k - 1))
        for r in range(1, rows):
            land(k, r)
        for side, (src, valid) in enumerate(spots(k)):

            @pl.when(valid)
            def _():
                norm_rows(src)
                update(inner, src)

        return 0

    lax.fori_loop(1, chips, hop, 0)

    def close(chunk):
        _, y, _, count = chunk
        return dot((y[...] / count[...]).astype(BF), wvo[...])

    o = close(inner)
    for r in range(rows):
        own[1 + r] = (every[mine + r].astype(F32) + o[r * width : (r + 1) * width]).astype(BF)
    for back in (0, 1):

        @pl.when(here.has_next & (here.c == back))
        def _():
            for copy_row in across[:: 1 - 2 * back]:
                copy_row.start()

    if chips < 3:
        outer_start()
    if chips > 1:
        outer_update(chips - 1)
    o = close(outer)
    for ok, row, at in edges:
        slot = at * (rows + 1)

        @pl.when(ok)
        def _():
            own[slot] = (every[row].astype(F32) + o[at * width : (at + 1) * width]).astype(BF)

        @pl.when(jnp.logical_not(ok))
        def _():
            own[slot] = jnp.zeros((width, ch), BF)

    def drain():
        def each(k, _):
            for side, (src, valid) in enumerate(spots(k)):

                @pl.when(valid & sides[side][1])
                def _():
                    for r in range(rows):
                        copy(src * rows + r, side).wait_send()

            return 0

        lax.fori_loop(0, chips, each, 0)

    return drain


def last_part(
    here, own, cache, gain, wup, wlow_hbm, out, across,
    x, acc, wlow, prior, chalo, wfull, wmix, wtap, grid, upper, flat,
    ps, pr, cs, cr, ws, wr, ls, fs, es, er, us, ur,
):
    frames = cache.shape[0]
    height, width, ch = own.shape
    c, z = here.c, here.z
    tall = cache.shape[1]
    low = cache.shape[2]
    wide = cache.shape[3]
    two = 2 * low
    part = wup.shape[2]
    first = jnp.logical_not(here.has_prev)
    fetch = pltpu.make_async_copy(wlow_hbm, wlow, fs)
    fetch.start()
    local = pltpu.make_async_copy(wup, wfull.at[c], ls)
    local.start()
    relays = (
        (0, here.up, remote(prior.at[1], prior.at[height - 1], ps.at[0], pr.at[0], {"rows": z - 1})),
        (height - 3, here.down, remote(prior.at[height - 2], prior.at[0], ps.at[1], pr.at[1], {"rows": z + 1})),
    )
    to_up = remote(cache.at[:, 0], chalo.at[1], cs.at[0], cr.at[0], {"rows": z - 1})
    to_down = remote(cache.at[:, tall - 1], chalo.at[0], cs.at[1], cr.at[1], {"rows": z + 1})
    weights = remote(wup, wfull.at[c], ws, wr, {"chan": 1 - c})

    weights.start()
    yield
    for edge, inside in ((0, here.up), (own.shape[0] - 1, here.down)):

        @pl.when(jnp.logical_not(inside))
        def _():
            prior[edge] = jnp.zeros(own.shape[1:], BF)

    taps_t, taps_h = wlow.shape[:2]
    fetch.wait()

    def lay(i, _):
        kt, kh = i // taps_h, i % taps_h
        tap = [wlow[kt, kh, k * low : (k + 1) * low] for k in range(3)]
        none = jnp.zeros((low, part), BF)
        blocks = ((tap[1], tap[0]), (tap[2], tap[1]), (none, tap[2]), (tap[0], none))
        for at, (even, odd) in enumerate(blocks):
            wtap[kt, kh, at * low : (at + 1) * low, :] = jnp.concatenate([even, odd], axis=1)
        return 0

    lax.fori_loop(0, taps_t * taps_h, lay, 0)

    local.wait()
    weights.wait_recv()
    groups = (((0, 1), (2,)), ((0,), (1, 2)))
    columns = ((1, 2), (0, 1), (0,), (2,))
    for parity, slots in enumerate(groups):
        for slot, khs in enumerate(slots):
            for half in (0, 1):
                by_kw = [sum(wfull[half, kh, kw].astype(F32) for kh in khs) for kw in range(3)]
                for at, kws in enumerate(columns):
                    start = at * low + half * part
                    wmix[parity, start : start + part, slot * ch : (slot + 1) * ch] = sum(by_kw[kw] for kw in kws).astype(BF)

    yield
    pl.when(first & here.up)(lambda: to_up.start())
    pl.when(first & here.down)(lambda: to_down.start())

    gains = gain[...].reshape(1, low)
    gains = jnp.concatenate([gains, gains], axis=1)
    lanes = 128
    starts = range(0, two, lanes)
    lane = lax.broadcasted_iota(jnp.int32, (width, lanes), 1)
    col = lax.broadcasted_iota(jnp.int32, (width, lanes), 0)

    def choose(start, first, last):
        if start + lanes <= low:
            return first()
        if start >= low:
            return last()
        return jnp.where(lane + start < low, first(), last())

    def prev(v):
        return jnp.where(col == 0, 0.0, pltpu.roll(v, 1, 0))

    def following(v):
        return jnp.where(col == width - 1, 0.0, pltpu.roll(v, width - 1, 0))

    def cut_up(v):
        return [v[:, a : a + lanes] for a in starts]

    def beside(slot, row, pieces):
        for a, v in zip(starts, pieces):
            x[slot, tall + 2 + row, :, a : a + lanes] = choose(a, lambda: following(v), lambda: prev(v)).astype(BF)

    def put(slot, row, pieces):
        for a, v in zip(starts, pieces):
            x[slot, row, :, a : a + lanes] = v.astype(BF)
        beside(slot, row, pieces)

    def row_copy(slot, at, r):
        piece = x.at[slot, r]
        return remote(piece, piece, es.at[at, r], er.at[at, r], {"chan": 1 - c})

    def upper_copy(f, r):
        return remote(upper.at[f, r], upper.at[f, r], us.at[r], ur.at[r], {"chan": 1 - c})

    def raise_frame(tile, at):
        slot = at * frames + c
        n = height - 1
        pairs = jnp.concatenate([tile[0:n], tile[1 : n + 1]], axis=2).reshape(n * width, 2 * ch)
        for parity in (0, 1):
            grid[parity] = dot_t(pairs, wmix[parity]).reshape(n, width, 2 * two)
        for r in range(tall + 2):
            same, cross = grid[r % 2, r // 2, :, :two], grid[r % 2, r // 2, :, two:]
            vs = [
                (v + choose(a, lambda: prev(u), lambda: following(u))).astype(BF)
                for a, v, u in zip(starts, cut_up(same), cut_up(cross))
            ]
            if at and 0 < r <= tall:
                for a, v in zip(starts, vs):
                    upper[c, r - 1, :, a : a + lanes] = v
                upper_copy(c, r - 1).start()
            vs = [v.astype(F32) for v in vs]
            zero = jnp.zeros((width, lanes), F32)
            mean_even = sum(choose(a, lambda: v * v, lambda: zero) for a, v in zip(starts, vs) if a < low)
            mean_odd = sum(choose(a, lambda: zero, lambda: v * v) for a, v in zip(starts, vs) if a + lanes > low)
            by_even, by_odd = (
                lax.rsqrt(jnp.sum(m, axis=-1, keepdims=True) / low + 1e-06) for m in (mean_even, mean_odd)
            )
            vs = [
                silu(v * choose(a, lambda: by_even, lambda: by_odd) * gains[:, a : a + lanes]) for a, v in zip(starts, vs)
            ]
            if r == 0:
                vs = [jnp.where(here.up, v, 0.0) for v in vs]
            if r == tall + 1:
                vs = [jnp.where(here.down, v, 0.0) for v in vs]
            put(slot, r, vs)
            row_copy(slot, at, r).start()

    def land(at):
        other = at * frames + 1 - c
        for r in range(tall + 2):
            row_copy(other, at, r).wait_recv()
            beside(other, r, cut_up(x[other, r].astype(F32)))

    raise_frame(own, 1)

    @pl.when(here.has_prev)
    def _():
        for back in (0, 1):

            @pl.when(c == back)
            def _():
                for r in range(len(across))[:: 1 - 2 * back]:
                    across[r].wait_recv()
                    for at, ok, relay in relays:
                        if at == r:
                            pl.when(ok)(lambda: relay.start())

    n = 2 * part
    pick = picker(two, n, lambda k, j: k == jnp.where(j < part, j, j - part + low) + c * part)
    for r in range(tall):
        upper_copy(1 - c, r).wait_recv()
    acc[...] = dot(upper[...].reshape(-1, two), pick)

    def run_taps(at, pair, before):
        def each(i, _):
            turned = c * (2 if at else 1)
            e = (i + turned) % taps_t
            t, kt = pair(e)
            own_first = 1 + (1 - c if at else c)
            pl.when(before & (i == own_first))(lambda: land(at))
            block = pl.ds(pl.multiple_of(t * tall * width, tall * width), tall * width)

            def tap(kh, _):
                v = jnp.concatenate([x[t + kt, pl.ds(k * (tall + 2) + kh, tall)] for k in (0, 1)], axis=2)
                acc[block, :] += dot(v.reshape(tall * width, 2 * two), wtap[kt, kh])
                return 0

            for kh in range(taps_h):
                tap(kh, 0)
            return 0

        lax.fori_loop(0, taps_t, each, 0)

    run_taps(1, lambda e: ((e + 1) // 2, 2 - e % 2), c >= 0)

    @pl.when(here.has_prev)
    def _():
        pl.when(here.down)(lambda: relays[0][2].wait_recv())
        pl.when(here.up)(lambda: relays[1][2].wait_recv())
        raise_frame(prior, 0)

    spots = [picker(width, wide, lambda k, n: n == 2 * k + p) for p in (0, 1)]

    def take(slot, row, flipped):
        put(slot, row, cut_up(jnp.concatenate([dot_t(spot, flipped) for spot in spots], axis=1)))

    @pl.when(first)
    def _():
        def each(i, _):
            take(i // tall, 1 + i % tall, cache[i // tall, i % tall])
            return 0

        lax.fori_loop(0, frames * tall, each, 0)

    for row, inside, k, copy in ((0, here.up, 0, to_down), (tall + 1, here.down, 1, to_up)):

        @pl.when(first & inside)
        def _():
            copy.wait_recv()
            for f in range(frames):
                take(f, row, chalo[k, f])

        @pl.when(first & jnp.logical_not(inside))
        def _():
            for f in range(frames):
                put(f, row, cut_up(jnp.zeros((width, two), F32)))

    run_taps(0, lambda e: (e // 2, e % 2), here.has_prev)

    def turn(i, _):
        done = acc[pl.ds(pl.multiple_of(i * width, width), width), :].T.astype(BF)
        for p in (0, 1):
            flat[p, i] = done[p * part : (p + 1) * part]
        return 0

    lax.fori_loop(0, frames * tall, turn, 0)
    for f in range(frames):
        sides = [flat[p, f * tall : (f + 1) * tall].reshape(tall * part, width) for p in (0, 1)]
        out[f] = (dot(sides[0], spots[0]) + dot(sides[1], spots[1])).astype(BF).reshape(tall, part, wide)
    weights.wait_send()
    for r in range(tall):
        upper_copy(c, r).wait_send()
    for r in range(tall + 2):
        row_copy(frames + c, 1, r).wait_send()

    @pl.when(here.has_prev)
    def _():
        for _, ok, relay in relays:
            pl.when(ok)(lambda: relay.wait_send())
        for r in range(tall + 2):
            row_copy(c, 0, r).wait_send()

    for copy in across:
        pl.when(here.has_next)(lambda: copy.wait_send())
    pl.when(first & here.up)(lambda: to_up.wait_send())
    pl.when(first & here.down)(lambda: to_down.wait_send())


def whole_kernel(counts, *refs):
    groups = []
    for count in counts:
        groups.append(refs[:count])
        refs = refs[count:]
    ins, (out,), shared, first, attn, last = groups
    latent, cache_mid, cache_low, gain_mid, gain_attn, gain_low, conv_mid, attn_qkv, attn_proj, conv_up, conv_low = ins
    every, own, prior, wqkv, wproj, wqk, wvo, low_cache, sems, xs, xr = shared
    fetches = [
        pltpu.make_async_copy(src, dst, sems.at[i])
        for i, (src, dst) in enumerate(((attn_qkv, wqkv), (attn_proj, wproj), (cache_low, low_cache)))
    ]
    here = Place()
    rows, ch = own.shape[0] - 2, own.shape[2]
    across = [
        remote(own.at[1 + r], prior.at[1 + r], xs.at[r], xr.at[r], {"segment": here.s + 1}) for r in range(rows)
    ]
    tail = last_part(here, own, low_cache, gain_low, conv_up, conv_low, out, across, *last[:2], last[2], prior, *last[3:])

    def begun():
        for fetch in fetches:
            fetch.start()
        next(tail)

    def fold():
        for fetch in fetches:
            fetch.wait()
        wqk[...] = (dot_t(wqkv[:, :ch], wqkv[:, ch : 2 * ch]) * (math.log2(math.e) / math.sqrt(ch))).astype(BF)
        wvo[...] = dot(wqkv[:, 2 * ch :], wproj[...]).astype(BF)

    drains = [first_part(here, latent, cache_mid, gain_mid, conv_mid, every, begun, fold, *first)]
    drains.append(attn_part(here, lambda: next(tail), gain_attn, wqk, wvo, every, own, across, *attn))
    next(tail, None)
    for drain in drains:
        drain()


def call(kernel, number, outs, scratch, *args, far=()):
    return pl.pallas_call(
        kernel,
        out_shape=outs,
        in_specs=[pl.BlockSpec(memory_space=pl.ANY if i in far else pltpu.VMEM) for i in range(len(args))],
        out_specs=jax.tree.map(lambda _: pl.BlockSpec(memory_space=pltpu.VMEM), outs),
        scratch_shapes=scratch,
        compiler_params=pltpu.CompilerParams(
            collective_id=number, has_side_effects=True, vmem_limit_bytes=67043328
        ),
    )(*args)


def body(
    latent, cache_mid, cache_low, gain_mid, gain_attn, gain_low, conv_mid, attn_qkv, attn_proj, conv_up, conv_low
):
    frames, rows, width, ch = latent.shape
    part = conv_mid.shape[-1]
    dma, one = pltpu.SemaphoreType.DMA, pltpu.SemaphoreType.DMA(())
    taps_t, taps_h, taps_w = conv_mid.shape[:3]
    total = rows * lax.axis_size("rows")
    cache_t = jnp.swapaxes(cache_low, 2, 3)
    tile = pltpu.VMEM((rows + 2, width, ch), BF)
    shared = [
        pltpu.VMEM((total, width, ch), BF), tile, tile,
        pltpu.VMEM(attn_qkv.shape, BF), pltpu.VMEM(attn_proj.shape, BF),
        pltpu.VMEM((ch, ch), BF), pltpu.VMEM((ch, ch), BF), pltpu.VMEM(cache_t.shape, BF),
        dma((3,)), dma((rows,)), dma((rows,)),
    ]
    first = [
        pltpu.VMEM(latent.shape, BF),
        pltpu.VMEM((taps_t - 1 + frames, rows, width, ch), BF),
        pltpu.VMEM((taps_t, taps_h, taps_w, part, ch), BF),
        pltpu.VMEM((taps_w, frames, rows + 2, width, part), F32),
        pltpu.VMEM((2, width, frames * part), BF),
        pltpu.VMEM((2, width, frames * part), BF),
        pltpu.VMEM((frames, rows, width, ch), BF),
        pltpu.VMEM((rows, width, ch), BF),
        dma((2,)), dma((2,)), *(dma((taps_t - 1,)) for _ in range(4)), one, one, dma((2,)), dma((taps_h,)),
    ]
    sizes = (rows * width, 2 * width)
    attn = [
        pltpu.VMEM((total, width, ch), BF),
        *(pltpu.VMEM((n, ch), BF) for n in sizes),
        *(pltpu.VMEM((n, ch), F32) for n in sizes),
        *(pltpu.VMEM((n, 1), F32) for n in sizes),
        *(pltpu.VMEM((n, 1), F32) for n in sizes),
        dma((total, 2)),
        dma((total,)),
    ]
    _, tall, wide, low = cache_low.shape
    cut = conv_low.shape[-1]
    two = 2 * low
    taps_t, taps_h, taps_w = conv_low.shape[:3]
    last = [
        pltpu.VMEM((2 * frames, 2 * (tall + 2), width, two), BF),
        pltpu.VMEM((frames * tall * width, 2 * cut), F32),
        pltpu.VMEM((taps_t, taps_h, taps_w * low, cut), BF),
        pltpu.VMEM((2, frames, low, wide), BF),
        pltpu.VMEM((2, 3, 3, cut, ch), BF),
        pltpu.VMEM((2, 2 * two, 2 * ch), BF),
        pltpu.VMEM((taps_t, taps_h, 2 * two, 2 * cut), BF),
        pltpu.VMEM((2, rows + 1, width, 2 * two), F32),
        pltpu.VMEM((frames, tall, width, two), BF),
        pltpu.VMEM((2, frames * tall, cut, width), BF),
        dma((2,)), dma((2,)), dma((2,)), dma((2,)), one, one, one, one,
        dma((2, tall + 2)), dma((2, tall + 2)), dma((tall,)), dma((tall,)),
    ]
    args = (
        latent, cache_mid, cache_t, gain_mid, gain_attn, gain_low, jnp.swapaxes(conv_mid, 3, 4), attn_qkv, attn_proj,
        jnp.swapaxes(conv_up, 2, 3), conv_low.reshape(taps_t, taps_h, taps_w * low, cut),
    )
    counts = (len(args), 1, len(shared), len(first), len(attn), len(last))
    decoded = call(
        functools.partial(whole_kernel, counts),
        0,
        jax.ShapeDtypeStruct((frames, tall, cut, wide), BF),
        shared + first + attn + last,
        *args,
        far=(0, 1, 2, 6, 7, 8, 9, 10),
    )
    return jnp.swapaxes(decoded, 2, 3)


def solution(mesh):
    placed = (
        P(("groups", "segment"), "rows", None, None),
        P("groups", "rows", None, None),
        P("groups", "rows", None, None),
        P(),
        P(),
        P(),
        P(None, None, None, None, "chan"),
        P(),
        P(),
        P(None, None, None, "chan"),
        P(None, None, None, None, "chan"),
    )
    return jax.shard_map(
        body,
        mesh=mesh,
        in_specs=placed,
        out_specs=P(("groups", "segment"), "rows", None, "chan"),
        check_vma=False,
    )
```

```python
import functools
import math

import jax
import jax.numpy as jnp
from jax import lax
from jax.experimental import pallas as pl
from jax.experimental.pallas import tpu as pltpu
from jax.sharding import PartitionSpec as P

MESH = pl.DeviceIdType.MESH
BF = jnp.bfloat16
F32 = jnp.float32


class Place:
    def __init__(self):
        self.rows, self.segs = lax.axis_size("rows"), lax.axis_size("segment")
        self.z, self.s, self.c = (lax.axis_index(a) for a in ("rows", "segment", "chan"))
        self.up, self.down = self.z > 0, self.z < self.rows - 1
        self.has_next, self.has_prev = self.s < self.segs - 1, self.s > 0

    def greet(self):
        barrier = pltpu.get_barrier_semaphore()
        n = jnp.int32(1)
        pl.semaphore_signal(barrier, inc=1, device_id={"chan": 1 - self.c}, device_id_type=MESH)
        for ok, target in (
            (self.up, {"rows": self.z - 1}),
            (self.down, {"rows": self.z + 1}),
            (self.has_next, {"segment": self.s + 1}),
            (self.has_prev, {"segment": self.s - 1}),
        ):

            @pl.when(ok)
            def _():
                pl.semaphore_signal(barrier, inc=1, device_id=target, device_id_type=MESH)

            n = n + ok.astype(jnp.int32)
        return lambda: pl.semaphore_wait(barrier, n)


def remote(src, dst, send, recv, target):
    return pltpu.make_async_remote_copy(
        src_ref=src, dst_ref=dst, send_sem=send, recv_sem=recv, device_id=target, device_id_type=MESH
    )


def normed(v, gain):
    return v * lax.rsqrt(jnp.mean(v * v, axis=-1, keepdims=True) + 1e-06) * gain


def silu(v):
    return 0.5 * v * (1.0 + jnp.tanh(0.5 * v))


def dot(a, b):
    return jnp.dot(a, b, preferred_element_type=F32)


def dot_t(a, b):
    return lax.dot_general(a, b, (((1,), (1,)), ((), ())), preferred_element_type=F32)


def picker(rows, cols, hit):
    k = lax.broadcasted_iota(jnp.int32, (rows, cols), 0)
    n = lax.broadcasted_iota(jnp.int32, (rows, cols), 1)
    return jnp.where(hit(k, n), 1.0, 0.0).astype(BF)


def first_part(
    here, latent_hbm, cache_hbm, gain_mid, w_hbm, every, begun, later,
    latent, xa, w, acc, edge_out, edge_in, seg, got, es, er, xs, xr, ps, pr, gs, gr, ls, wsem,
):
    frames, rows, width, ch = latent.shape
    taps_t, taps_h, taps_w, part = w.shape[:4]
    before = taps_t - 1
    c, z = here.c, here.z
    first = jnp.logical_not(here.has_prev)
    order = (2, 0, 1)
    met = here.greet()
    own = pltpu.make_async_copy(latent_hbm, latent, ls.at[0])
    local = pltpu.make_async_copy(cache_hbm, xa.at[pl.ds(0, before)], ls.at[1])
    weights = [pltpu.make_async_copy(w_hbm.at[:, kh], w.at[:, kh], wsem.at[kh]) for kh in order]
    own.start()
    pl.when(first)(lambda: local.start())
    for fetch in weights:
        fetch.start()
    acc[...] = jnp.zeros(acc.shape, F32)
    half = rows // 2

    def piece(f):
        return xa.at[f, pl.ds(c * half, half)]

    across = [remote(piece(before + f), piece(f), xs.at[f], xr.at[f], {"segment": here.s + 1}) for f in range(before)]
    share = [remote(piece(f), piece(f), ps.at[f], pr.at[f], {"chan": 1 - c}) for f in range(before)]
    to_up, to_down = (
        [remote(edge_out.at[k, t], edge_in.at[1 - k, t], es.at[k, t], er.at[1 - k, t], {"rows": z + side}) for t in range(frames)]
        for k, side in ((0, -1), (1, 1))
    )
    swap = remote(seg.at[1 - c], got, gs, gr, {"chan": 1 - c})

    own.wait()
    gain = gain_mid[...].reshape(1, ch)

    def fill(f, side):
        for r in range(half):
            row = side * half + r
            xa[before + f, row] = silu(normed(latent[f, row].astype(F32), gain)).astype(BF)

    late = tuple(range(before))[::-1]
    fill(late[0], c)
    met()
    for f in late:
        if f != late[0]:
            fill(f, c)
        pl.when(here.has_next)(lambda: across[f].start())
    begun()
    for f in range(frames):
        fill(f, 1 - c)
    pick = picker(ch, part, lambda k, n: k == n + c * part)
    for t in range(frames):
        acc[1, t, 1 : 1 + rows] = dot(latent[t].reshape(rows * width, ch), pick).reshape(rows, width, part)

    def taps(kh, *uses):
        for t, some in uses:
            left = jnp.concatenate([xa[t + kt].reshape(rows * width, ch) for kt in some], axis=1)
            for kw in range(taps_w):
                right = jnp.concatenate([w[kt, kh, kw] for kt in some], axis=1)
                acc[kw, t, 2 - kh : 2 - kh + rows] += dot_t(left, right).reshape(rows, width, part)

    def uses(frames_in):
        return [(t, some) for t in range(frames) if (some := [kt for kt in range(taps_t) if t + kt in frames_in])]

    fresh = uses(range(before, before + frames))
    stale = uses(range(before))
    col = lax.broadcasted_iota(jnp.int32, (width, part), 0)

    def joined(t, row):
        left = jnp.where(col == 0, 0.0, pltpu.roll(acc[0, t, row], 1, 0))
        right = jnp.where(col == width - 1, 0.0, pltpu.roll(acc[2, t, row], width - 1, 0))
        return acc[1, t, row] + left + right

    def send_edges(t):
        for k, row in enumerate((0, rows + 1)):
            v = joined(t, row)
            edge_out[k, t] = jnp.concatenate([v[: width // 2], v[width // 2 :]], axis=1).astype(BF)
        pl.when(here.up)(lambda: to_up[t].start())
        pl.when(here.down)(lambda: to_down[t].start())

    def all_taps(kh, low, high):
        n = frames * (high - low) * width
        left = jnp.concatenate([xa[kt : kt + frames, low:high].reshape(n, ch) for kt in range(taps_t)], axis=1)

        for kw in range(taps_w):
            right = jnp.concatenate([w[kt, kh, kw] for kt in range(taps_t)], axis=1)
            acc[kw, :, low + 2 - kh : high + 2 - kh] += dot_t(left, right).reshape(frames, high - low, width, part)

    for fetch in weights[:2]:
        fetch.wait()

    @pl.when(first)
    def _():
        local.wait()
        all_taps(2, 0, 1)
        all_taps(0, rows - 1, rows)
        for t in late:
            send_edges(t)
        all_taps(2, 1, rows)
        all_taps(0, 0, rows - 1)
        weights[2].wait()
        all_taps(1, 0, rows)

    @pl.when(here.has_prev)
    def _():
        for kh in order[:2]:
            taps(kh, *fresh)
        weights[2].wait()
        taps(order[2], *fresh)
        for f in late:
            across[f].wait_recv()
            share[f].start()
            share[f].wait_recv()
            for kh in order[:2]:
                taps(kh, *uses((f,)))
            send_edges(f)
        taps(order[2], *stale)

    later()
    for ok, copy, k, row in ((here.up, to_down, 0, 1), (here.down, to_up, 1, rows)):

        @pl.when(ok)
        def _():
            for t in late:
                copy[t].wait_recv()
                got_edge = edge_in[k, t].astype(F32)
                for at in (0, 1):
                    block = slice(at * width // 2, (at + 1) * width // 2)
                    acc[1, t, row, block] += got_edge[:, at * part : (at + 1) * part]

    def finish(t):
        for r in range(rows):
            v = joined(t, 1 + r)
            seg[t, r] = jnp.concatenate([v, v], axis=1).astype(BF)

    finish(1 - c)
    swap.start()
    finish(c)
    lower = lax.broadcasted_iota(jnp.int32, (width, ch), 1) < part
    kept = lower == (c == 0)
    swap.wait_recv()
    for r in range(rows):
        every[z * rows + r] = jnp.where(kept, seg[c, r].astype(F32), got[r].astype(F32)).astype(BF)

    def drain():
        swap.wait_send()
        for f in late:
            pl.when(here.has_prev)(lambda: share[f].wait_send())
            pl.when(here.has_next)(lambda: across[f].wait_send())
        for t in range(frames):
            pl.when(here.up)(lambda: to_up[t].wait_send())
            pl.when(here.down)(lambda: to_down[t].wait_send())

    return drain


def attn_part(
    here, later, gain_attn, wqk, wvo, every, own, across,
    keys, q_own, q_edge, y_own, y_edge, top_own, top_edge, sum_own, sum_edge, send, recv,
):
    total, width, ch = every.shape
    z, chips = here.z, here.rows
    rows = total // chips
    mine = z * rows
    gain = gain_attn[...].reshape(1, ch)
    sides = ((-1, here.down, {"rows": z + 1}), (1, here.up, {"rows": z - 1}))

    def copy(row, side):
        return remote(every.at[row], every.at[row], send.at[row, side], recv.at[row], sides[side][2])

    def turn(side, r):
        return r if side else rows - 1 - r

    for r in range(rows):
        for side, (_, ok, _) in enumerate(sides):
            pl.when(ok)(lambda: copy(mine + turn(side, r), side).start())

    def norm_rows(src):
        for r in range(rows):
            keys[src * rows + r] = normed(every[src * rows + r].astype(F32), gain).astype(BF)

    def update(chunk, src, count=1):
        q, y, top, total = chunk
        some = keys[pl.ds(src * rows, count * rows)].reshape(count * rows * width, ch)
        s = dot_t(q[...], some)
        high = jnp.maximum(top[...], jnp.max(s, axis=-1, keepdims=True))
        p = jnp.exp2(s - high)
        fade = jnp.exp2(top[...] - high)
        top[...] = high
        total[...] = total[...] * fade + jnp.sum(p, axis=-1, keepdims=True)
        y[...] = y[...] * fade + dot(p.astype(BF), some)

    inner = (q_own, y_own, top_own, sum_own)
    outer = (q_edge, y_edge, top_edge, sum_edge)
    for _, y, top, count in (inner, outer):
        y[...] = jnp.zeros(y.shape, F32)
        top[...] = jnp.full(top.shape, -jnp.inf, F32)
        count[...] = jnp.zeros(count.shape, F32)
    norm_rows(z)
    q_own[...] = dot(keys[pl.ds(mine, rows)].reshape(rows * width, ch), wqk[...]).astype(BF)
    later()
    edges = ((here.up, mine - 1, 0), (here.down, mine + rows, 1))

    def spots(k):
        return ((z - k, z - k >= 0), (z + k, z + k < chips))

    def outer_update(k):
        for src, valid in spots(k):
            pl.when(valid)(lambda: update(outer, src))

    def outer_start():
        for ok, row, at in edges:
            part = pl.ds(at * width, width)

            @pl.when(ok)
            def _():
                q_edge[part, :] = dot(keys[row], wqk[...]).astype(BF)

            @pl.when(jnp.logical_not(ok))
            def _():
                q_edge[part, :] = jnp.zeros((width, ch), BF)

        nearby(outer)

    def nearby(chunk):
        inside = here.up & here.down
        if chips > 2:
            pl.when(inside)(lambda: update(chunk, z - 1, 3))
        if chips > 1:
            pl.when(jnp.logical_not(inside))(lambda: update(chunk, z - here.up.astype(jnp.int32), 2))
        else:
            update(chunk, z)

    def land(k, r):
        for side, (src, valid) in enumerate(spots(k)):

            @pl.when(valid)
            def _():
                row = src * rows + turn(side, r)
                copy(row, side).wait_recv()
                pl.when(sides[side][1])(lambda: copy(row, side).start())

    def hop(k, _):
        land(k, 0)
        pl.when(k == 2)(outer_start)
        pl.when(k > 2)(lambda: outer_update(k - 1))
        for r in range(1, rows):
            land(k, r)
        for src, valid in spots(k):

            @pl.when(valid)
            def _():
                norm_rows(src)
                pl.when(k > 1)(lambda: update(inner, src))

        pl.when(k == 1)(lambda: nearby(inner))
        return 0

    lax.fori_loop(1, chips, hop, 0)
    if chips < 2:
        nearby(inner)

    def close(chunk):
        _, y, _, count = chunk
        return dot((y[...] / count[...]).astype(BF), wvo[...])

    o = close(inner)
    for r in range(rows):
        own[1 + r] = (every[mine + r].astype(F32) + o[r * width : (r + 1) * width]).astype(BF)
    for back in (0, 1):

        @pl.when(here.has_next & (here.c == back))
        def _():
            for copy_row in across[:: 1 - 2 * back]:
                copy_row.start()

    if chips < 3:
        outer_start()
    else:
        outer_update(chips - 1)
    o = close(outer)
    for ok, row, at in edges:
        slot = at * (rows + 1)

        @pl.when(ok)
        def _():
            own[slot] = (every[row].astype(F32) + o[at * width : (at + 1) * width]).astype(BF)

        @pl.when(jnp.logical_not(ok))
        def _():
            own[slot] = jnp.zeros((width, ch), BF)

    def drain():
        def each(k, _):
            for side, (src, valid) in enumerate(spots(k)):

                @pl.when(valid & sides[side][1])
                def _():
                    for r in range(rows):
                        copy(src * rows + r, side).wait_send()

            return 0

        lax.fori_loop(0, chips, each, 0)

    return drain


def last_part(
    here, own, cache, gain, wup, wlow_hbm, out, across,
    x, acc, wlow, prior, chalo, wfull, wmix, wtap, grid, upper, flat,
    ps, pr, cs, cr, ws, wr, ls, fs, es, er, us, ur,
):
    frames = cache.shape[0]
    height, width, ch = own.shape
    c, z = here.c, here.z
    tall = cache.shape[1]
    low = cache.shape[2]
    wide = cache.shape[3]
    two = 2 * low
    part = wup.shape[2]
    first = jnp.logical_not(here.has_prev)
    fetch = pltpu.make_async_copy(wlow_hbm, wlow, fs)
    fetch.start()
    local = pltpu.make_async_copy(wup, wfull.at[c], ls)
    local.start()
    relays = (
        (0, here.up, remote(prior.at[1], prior.at[height - 1], ps.at[0], pr.at[0], {"rows": z - 1})),
        (height - 3, here.down, remote(prior.at[height - 2], prior.at[0], ps.at[1], pr.at[1], {"rows": z + 1})),
    )
    to_up = remote(cache.at[:, 0], chalo.at[1], cs.at[0], cr.at[0], {"rows": z - 1})
    to_down = remote(cache.at[:, tall - 1], chalo.at[0], cs.at[1], cr.at[1], {"rows": z + 1})
    weights = remote(wup, wfull.at[c], ws, wr, {"chan": 1 - c})

    weights.start()
    yield
    for edge, inside in ((0, here.up), (own.shape[0] - 1, here.down)):

        @pl.when(jnp.logical_not(inside))
        def _():
            prior[edge] = jnp.zeros(own.shape[1:], BF)

    taps_t, taps_h = wlow.shape[:2]
    fetch.wait()

    def lay(i, _):
        kt, kh = i // taps_h, i % taps_h
        tap = [wlow[kt, kh, k * low : (k + 1) * low] for k in range(3)]
        none = jnp.zeros((low, part), BF)
        blocks = ((tap[1], tap[0]), (tap[2], tap[1]), (none, tap[2]), (tap[0], none))
        for at, (even, odd) in enumerate(blocks):
            wtap[kt, kh, at * low : (at + 1) * low, :] = jnp.concatenate([even, odd], axis=1)
        return 0

    lax.fori_loop(0, taps_t * taps_h, lay, 0)

    local.wait()
    weights.wait_recv()
    groups = (((0, 1), (2,)), ((0,), (1, 2)))
    columns = ((1, 2), (0, 1), (0,), (2,))
    for parity, slots in enumerate(groups):
        for slot, khs in enumerate(slots):
            for half in (0, 1):
                by_kw = [sum(wfull[half, kh, kw].astype(F32) for kh in khs) for kw in range(3)]
                for at, kws in enumerate(columns):
                    start = at * low + half * part
                    wmix[parity, start : start + part, slot * ch : (slot + 1) * ch] = sum(by_kw[kw] for kw in kws).astype(BF)

    yield
    pl.when(first & here.up)(lambda: to_up.start())
    pl.when(first & here.down)(lambda: to_down.start())

    gains = gain[...].reshape(1, low)
    gains = jnp.concatenate([gains, gains], axis=1)
    lanes = 128
    starts = range(0, two, lanes)
    lane = lax.broadcasted_iota(jnp.int32, (width, lanes), 1)
    col = lax.broadcasted_iota(jnp.int32, (width, lanes), 0)

    def choose(start, first, last):
        if start + lanes <= low:
            return first()
        if start >= low:
            return last()
        return jnp.where(lane + start < low, first(), last())

    def prev(v):
        return jnp.where(col == 0, 0.0, pltpu.roll(v, 1, 0))

    def following(v):
        return jnp.where(col == width - 1, 0.0, pltpu.roll(v, width - 1, 0))

    def cut_up(v):
        return [v[:, a : a + lanes] for a in starts]

    def beside(slot, row, pieces):
        for a, v in zip(starts, pieces):
            x[slot, tall + 2 + row, :, a : a + lanes] = choose(a, lambda: following(v), lambda: prev(v)).astype(BF)

    def put(slot, row, pieces):
        for a, v in zip(starts, pieces):
            x[slot, row, :, a : a + lanes] = v.astype(BF)
        beside(slot, row, pieces)

    def row_copy(slot, at, r):
        piece = x.at[slot, r]
        return remote(piece, piece, es.at[at, r], er.at[at, r], {"chan": 1 - c})

    def upper_copy(f, r):
        return remote(upper.at[f, r], upper.at[f, r], us.at[r], ur.at[r], {"chan": 1 - c})

    def raise_frame(tile, at):
        slot = at * frames + c
        n = height - 1
        pairs = jnp.concatenate([tile[0:n], tile[1 : n + 1]], axis=2).reshape(n * width, 2 * ch)
        for parity in (0, 1):
            grid[parity] = dot_t(pairs, wmix[parity]).reshape(n, width, 2 * two)
        for r in range(tall + 2):
            same, cross = grid[r % 2, r // 2, :, :two], grid[r % 2, r // 2, :, two:]
            vs = [
                (v + choose(a, lambda: prev(u), lambda: following(u))).astype(BF)
                for a, v, u in zip(starts, cut_up(same), cut_up(cross))
            ]
            if at and 0 < r <= tall:
                for a, v in zip(starts, vs):
                    upper[c, r - 1, :, a : a + lanes] = v
                upper_copy(c, r - 1).start()
            vs = [v.astype(F32) for v in vs]
            zero = jnp.zeros((width, lanes), F32)
            mean_even = sum(choose(a, lambda: v * v, lambda: zero) for a, v in zip(starts, vs) if a < low)
            mean_odd = sum(choose(a, lambda: zero, lambda: v * v) for a, v in zip(starts, vs) if a + lanes > low)
            by_even, by_odd = (
                lax.rsqrt(jnp.sum(m, axis=-1, keepdims=True) / low + 1e-06) for m in (mean_even, mean_odd)
            )
            vs = [
                silu(v * choose(a, lambda: by_even, lambda: by_odd) * gains[:, a : a + lanes]) for a, v in zip(starts, vs)
            ]
            if r == 0:
                vs = [jnp.where(here.up, v, 0.0) for v in vs]
            if r == tall + 1:
                vs = [jnp.where(here.down, v, 0.0) for v in vs]
            put(slot, r, vs)
            row_copy(slot, at, r).start()

    def land(at):
        other = at * frames + 1 - c
        for r in range(tall + 2):
            row_copy(other, at, r).wait_recv()
            beside(other, r, cut_up(x[other, r].astype(F32)))

    raise_frame(own, 1)

    @pl.when(here.has_prev)
    def _():
        for back in (0, 1):

            @pl.when(c == back)
            def _():
                for r in range(len(across))[:: 1 - 2 * back]:
                    across[r].wait_recv()
                    for at, ok, relay in relays:
                        if at == r:
                            pl.when(ok)(lambda: relay.start())

    n = 2 * part
    pick = picker(two, n, lambda k, j: k == jnp.where(j < part, j, j - part + low) + c * part)
    for r in range(tall):
        upper_copy(1 - c, r).wait_recv()
    acc[...] = dot(upper[...].reshape(-1, two), pick)

    def run_taps(at, pair, before):
        def each(i, _):
            turned = c * (2 if at else 1)
            e = (i + turned) % taps_t
            t, kt = pair(e)
            own_first = 1 + (1 - c if at else c)
            pl.when(before & (i == own_first))(lambda: land(at))
            block = pl.ds(pl.multiple_of(t * tall * width, tall * width), tall * width)

            def tap(kh, _):
                v = jnp.concatenate([x[t + kt, pl.ds(k * (tall + 2) + kh, tall)] for k in (0, 1)], axis=2)
                acc[block, :] += dot(v.reshape(tall * width, 2 * two), wtap[kt, kh])
                return 0

            for kh in range(taps_h):
                tap(kh, 0)
            return 0

        lax.fori_loop(0, taps_t, each, 0)

    run_taps(1, lambda e: ((e + 1) // 2, 2 - e % 2), c >= 0)

    @pl.when(here.has_prev)
    def _():
        pl.when(here.down)(lambda: relays[0][2].wait_recv())
        pl.when(here.up)(lambda: relays[1][2].wait_recv())
        raise_frame(prior, 0)

    spots = [picker(width, wide, lambda k, n: n == 2 * k + p) for p in (0, 1)]

    def take(slot, row, flipped):
        put(slot, row, cut_up(jnp.concatenate([dot_t(spot, flipped) for spot in spots], axis=1)))

    @pl.when(first)
    def _():
        def each(i, _):
            take(i // tall, 1 + i % tall, cache[i // tall, i % tall])
            return 0

        lax.fori_loop(0, frames * tall, each, 0)

    for row, inside, k, copy in ((0, here.up, 0, to_down), (tall + 1, here.down, 1, to_up)):

        @pl.when(first & inside)
        def _():
            copy.wait_recv()
            for f in range(frames):
                take(f, row, chalo[k, f])

        @pl.when(first & jnp.logical_not(inside))
        def _():
            for f in range(frames):
                put(f, row, cut_up(jnp.zeros((width, two), F32)))

    run_taps(0, lambda e: (e // 2, e % 2), here.has_prev)

    def turn(i, _):
        done = acc[pl.ds(pl.multiple_of(i * width, width), width), :].astype(BF).T
        for p in (0, 1):
            flat[p, i] = done[p * part : (p + 1) * part]
        return 0

    lax.fori_loop(0, frames * tall, turn, 0)
    for f in range(frames):
        sides = [flat[p, f * tall : (f + 1) * tall].reshape(tall * part, width) for p in (0, 1)]
        out[f] = (dot(sides[0], spots[0]) + dot(sides[1], spots[1])).astype(BF).reshape(tall, part, wide)
    weights.wait_send()
    for r in range(tall):
        upper_copy(c, r).wait_send()
    for r in range(tall + 2):
        row_copy(frames + c, 1, r).wait_send()

    @pl.when(here.has_prev)
    def _():
        for _, ok, relay in relays:
            pl.when(ok)(lambda: relay.wait_send())
        for r in range(tall + 2):
            row_copy(c, 0, r).wait_send()

    for copy in across:
        pl.when(here.has_next)(lambda: copy.wait_send())
    pl.when(first & here.up)(lambda: to_up.wait_send())
    pl.when(first & here.down)(lambda: to_down.wait_send())


def whole_kernel(counts, *refs):
    groups = []
    for count in counts:
        groups.append(refs[:count])
        refs = refs[count:]
    ins, (out,), shared, first, attn, last = groups
    latent, cache_mid, cache_low, gain_mid, gain_attn, gain_low, conv_mid, attn_qkv, attn_proj, conv_up, conv_low = ins
    every, own, prior, wqkv, wproj, wqk, wvo, low_cache, sems, xs, xr = shared
    fetches = [
        pltpu.make_async_copy(src, dst, sems.at[i])
        for i, (src, dst) in enumerate(((attn_qkv, wqkv), (attn_proj, wproj), (cache_low, low_cache)))
    ]
    here = Place()
    rows, ch = own.shape[0] - 2, own.shape[2]
    across = [
        remote(own.at[1 + r], prior.at[1 + r], xs.at[r], xr.at[r], {"segment": here.s + 1}) for r in range(rows)
    ]
    tail = last_part(here, own, low_cache, gain_low, conv_up, conv_low, out, across, *last[:2], last[2], prior, *last[3:])

    def begun():
        for fetch in fetches:
            fetch.start()
        next(tail)

    def fold():
        for fetch in fetches:
            fetch.wait()
        wqk[...] = (dot_t(wqkv[:, :ch], wqkv[:, ch : 2 * ch]) * (math.log2(math.e) / math.sqrt(ch))).astype(BF)
        wvo[...] = dot(wqkv[:, 2 * ch :], wproj[...]).astype(BF)

    drains = [first_part(here, latent, cache_mid, gain_mid, conv_mid, every, begun, fold, *first)]
    drains.append(attn_part(here, lambda: next(tail), gain_attn, wqk, wvo, every, own, across, *attn))
    next(tail, None)
    for drain in drains:
        drain()


def call(kernel, number, outs, scratch, *args, far=()):
    return pl.pallas_call(
        kernel,
        out_shape=outs,
        in_specs=[pl.BlockSpec(memory_space=pl.ANY if i in far else pltpu.VMEM) for i in range(len(args))],
        out_specs=jax.tree.map(lambda _: pl.BlockSpec(memory_space=pltpu.VMEM), outs),
        scratch_shapes=scratch,
        compiler_params=pltpu.CompilerParams(
            collective_id=number, has_side_effects=True, vmem_limit_bytes=67043328
        ),
    )(*args)


def body(
    latent, cache_mid, cache_low, gain_mid, gain_attn, gain_low, conv_mid, attn_qkv, attn_proj, conv_up, conv_low
):
    frames, rows, width, ch = latent.shape
    part = conv_mid.shape[-1]
    dma, one = pltpu.SemaphoreType.DMA, pltpu.SemaphoreType.DMA(())
    taps_t, taps_h, taps_w = conv_mid.shape[:3]
    total = rows * lax.axis_size("rows")
    cache_t = jnp.swapaxes(cache_low, 2, 3)
    tile = pltpu.VMEM((rows + 2, width, ch), BF)
    shared = [
        pltpu.VMEM((total, width, ch), BF), tile, tile,
        pltpu.VMEM(attn_qkv.shape, BF), pltpu.VMEM(attn_proj.shape, BF),
        pltpu.VMEM((ch, ch), BF), pltpu.VMEM((ch, ch), BF), pltpu.VMEM(cache_t.shape, BF),
        dma((3,)), dma((rows,)), dma((rows,)),
    ]
    first = [
        pltpu.VMEM(latent.shape, BF),
        pltpu.VMEM((taps_t - 1 + frames, rows, width, ch), BF),
        pltpu.VMEM((taps_t, taps_h, taps_w, part, ch), BF),
        pltpu.VMEM((taps_w, frames, rows + 2, width, part), F32),
        pltpu.VMEM((2, frames, width // 2, 2 * part), BF),
        pltpu.VMEM((2, frames, width // 2, 2 * part), BF),
        pltpu.VMEM((frames, rows, width, ch), BF),
        pltpu.VMEM((rows, width, ch), BF),
        dma((2, frames)), dma((2, frames)), *(dma((taps_t - 1,)) for _ in range(4)), one, one, dma((2,)), dma((taps_h,)),
    ]
    sizes = (rows * width, 2 * width)
    attn = [
        pltpu.VMEM((total, width, ch), BF),
        *(pltpu.VMEM((n, ch), BF) for n in sizes),
        *(pltpu.VMEM((n, ch), F32) for n in sizes),
        *(pltpu.VMEM((n, 1), F32) for n in sizes),
        *(pltpu.VMEM((n, 1), F32) for n in sizes),
        dma((total, 2)),
        dma((total,)),
    ]
    _, tall, wide, low = cache_low.shape
    cut = conv_low.shape[-1]
    two = 2 * low
    taps_t, taps_h, taps_w = conv_low.shape[:3]
    last = [
        pltpu.VMEM((2 * frames, 2 * (tall + 2), width, two), BF),
        pltpu.VMEM((frames * tall * width, 2 * cut), F32),
        pltpu.VMEM((taps_t, taps_h, taps_w * low, cut), BF),
        pltpu.VMEM((2, frames, low, wide), BF),
        pltpu.VMEM((2, 3, 3, cut, ch), BF),
        pltpu.VMEM((2, 2 * two, 2 * ch), BF),
        pltpu.VMEM((taps_t, taps_h, 2 * two, 2 * cut), BF),
        pltpu.VMEM((2, rows + 1, width, 2 * two), F32),
        pltpu.VMEM((frames, tall, width, two), BF),
        pltpu.VMEM((2, frames * tall, cut, width), BF),
        dma((2,)), dma((2,)), dma((2,)), dma((2,)), one, one, one, one,
        dma((2, tall + 2)), dma((2, tall + 2)), dma((tall,)), dma((tall,)),
    ]
    args = (
        latent, cache_mid, cache_t, gain_mid, gain_attn, gain_low, jnp.swapaxes(conv_mid, 3, 4), attn_qkv, attn_proj,
        jnp.swapaxes(conv_up, 2, 3), conv_low.reshape(taps_t, taps_h, taps_w * low, cut),
    )
    counts = (len(args), 1, len(shared), len(first), len(attn), len(last))
    decoded = call(
        functools.partial(whole_kernel, counts),
        0,
        jax.ShapeDtypeStruct((frames, tall, cut, wide), BF),
        shared + first + attn + last,
        *args,
        far=(0, 1, 2, 6, 7, 8, 9, 10),
    )
    return jnp.swapaxes(decoded, 2, 3)


def solution(mesh):
    placed = (
        P(("groups", "segment"), "rows", None, None),
        P("groups", "rows", None, None),
        P("groups", "rows", None, None),
        P(),
        P(),
        P(),
        P(None, None, None, None, "chan"),
        P(),
        P(),
        P(None, None, None, "chan"),
        P(None, None, None, None, "chan"),
    )
    return jax.shard_map(
        body,
        mesh=mesh,
        in_specs=placed,
        out_specs=P(("groups", "segment"), "rows", None, "chan"),
        check_vma=False,
    )
```

```python
import functools
import math

import jax
import jax.numpy as jnp
from jax import lax
from jax.experimental import pallas as pl
from jax.experimental.pallas import tpu as pltpu
from jax.sharding import PartitionSpec as P

MESH = pl.DeviceIdType.MESH
BF = jnp.bfloat16
F32 = jnp.float32


class Place:
    def __init__(self):
        self.rows, self.segs = lax.axis_size("rows"), lax.axis_size("segment")
        self.z, self.s, self.c = (lax.axis_index(a) for a in ("rows", "segment", "chan"))
        self.up, self.down = self.z > 0, self.z < self.rows - 1
        self.has_next, self.has_prev = self.s < self.segs - 1, self.s > 0

    def greet(self):
        barrier = pltpu.get_barrier_semaphore()
        n = jnp.int32(1)
        pl.semaphore_signal(barrier, inc=1, device_id={"chan": 1 - self.c}, device_id_type=MESH)
        for ok, target in (
            (self.up, {"rows": self.z - 1}),
            (self.down, {"rows": self.z + 1}),
            (self.has_next, {"segment": self.s + 1}),
            (self.has_prev, {"segment": self.s - 1}),
        ):

            @pl.when(ok)
            def _():
                pl.semaphore_signal(barrier, inc=1, device_id=target, device_id_type=MESH)

            n = n + ok.astype(jnp.int32)
        return lambda: pl.semaphore_wait(barrier, n)


def remote(src, dst, send, recv, target):
    return pltpu.make_async_remote_copy(
        src_ref=src, dst_ref=dst, send_sem=send, recv_sem=recv, device_id=target, device_id_type=MESH
    )


def normed(v, gain):
    return v * lax.rsqrt(jnp.mean(v * v, axis=-1, keepdims=True) + 1e-06) * gain


def silu(v):
    return 0.5 * v * (1.0 + jnp.tanh(0.5 * v))


def dot(a, b):
    return jnp.dot(a, b, preferred_element_type=F32)


def dot_t(a, b):
    return lax.dot_general(a, b, (((1,), (1,)), ((), ())), preferred_element_type=F32)


def picker(rows, cols, hit):
    k = lax.broadcasted_iota(jnp.int32, (rows, cols), 0)
    n = lax.broadcasted_iota(jnp.int32, (rows, cols), 1)
    return jnp.where(hit(k, n), 1.0, 0.0).astype(BF)


def first_part(
    here, latent_hbm, cache_hbm, gain_mid, w_hbm, every, begun, later,
    latent, xa, w, acc, edge_out, edge_in, seg, got, es, er, xs, xr, ps, pr, gs, gr, ls, wsem,
):
    frames, rows, width, ch = latent.shape
    taps_t, taps_h, taps_w, part = w.shape[:4]
    before = taps_t - 1
    c, z = here.c, here.z
    first = jnp.logical_not(here.has_prev)
    order = (2, 0, 1)
    met = here.greet()
    own = pltpu.make_async_copy(latent_hbm, latent, ls.at[0])
    local = pltpu.make_async_copy(cache_hbm, xa.at[pl.ds(0, before)], ls.at[1])
    weights = [pltpu.make_async_copy(w_hbm.at[:, kh], w.at[:, kh], wsem.at[kh]) for kh in order]
    own.start()
    pl.when(first)(lambda: local.start())
    for fetch in weights:
        fetch.start()
    acc[...] = jnp.zeros(acc.shape, F32)
    half = rows // 2

    def piece(f):
        return xa.at[f, pl.ds(c * half, half)]

    across = [remote(piece(before + f), piece(f), xs.at[f], xr.at[f], {"segment": here.s + 1}) for f in range(before)]
    share = [remote(piece(f), piece(f), ps.at[f], pr.at[f], {"chan": 1 - c}) for f in range(before)]
    to_up, to_down = (
        [remote(edge_out.at[k, t], edge_in.at[1 - k, t], es.at[k, t], er.at[1 - k, t], {"rows": z + side}) for t in range(frames)]
        for k, side in ((0, -1), (1, 1))
    )
    swap = remote(seg.at[1 - c], got, gs, gr, {"chan": 1 - c})

    own.wait()
    gain = gain_mid[...].reshape(1, ch)

    def fill(f, side):
        for r in range(half):
            row = side * half + r
            xa[before + f, row] = silu(normed(latent[f, row].astype(F32), gain)).astype(BF)

    late = tuple(range(before))[::-1]
    fill(late[0], c)
    met()
    for f in late:
        if f != late[0]:
            fill(f, c)
        pl.when(here.has_next)(lambda: across[f].start())
    begun()
    for f in range(frames):
        fill(f, 1 - c)
    pick = picker(ch, part, lambda k, n: k == n + c * part)
    for t in range(frames):
        acc[1, t, 1 : 1 + rows] = dot(latent[t].reshape(rows * width, ch), pick).reshape(rows, width, part)

    def taps(kh, *uses):
        for t, some in uses:
            left = jnp.concatenate([xa[t + kt].reshape(rows * width, ch) for kt in some], axis=1)
            for kw in range(taps_w):
                right = jnp.concatenate([w[kt, kh, kw] for kt in some], axis=1)
                acc[kw, t, 2 - kh : 2 - kh + rows] += dot_t(left, right).reshape(rows, width, part)

    def uses(frames_in):
        return [(t, some) for t in range(frames) if (some := [kt for kt in range(taps_t) if t + kt in frames_in])]

    fresh = uses(range(before, before + frames))
    stale = uses(range(before))
    col = lax.broadcasted_iota(jnp.int32, (width, part), 0)

    def joined(t, row):
        left = jnp.where(col == 0, 0.0, pltpu.roll(acc[0, t, row], 1, 0))
        right = jnp.where(col == width - 1, 0.0, pltpu.roll(acc[2, t, row], width - 1, 0))
        return acc[1, t, row] + left + right

    def send_edges(t):
        for k, row in enumerate((0, rows + 1)):
            v = joined(t, row)
            edge_out[k, t] = jnp.concatenate([v[: width // 2], v[width // 2 :]], axis=1).astype(BF)
        pl.when(here.up)(lambda: to_up[t].start())
        pl.when(here.down)(lambda: to_down[t].start())

    def all_taps(kh, low, high):
        n = frames * (high - low) * width
        left = jnp.concatenate([xa[kt : kt + frames, low:high].reshape(n, ch) for kt in range(taps_t)], axis=1)

        for kw in range(taps_w):
            right = jnp.concatenate([w[kt, kh, kw] for kt in range(taps_t)], axis=1)
            acc[kw, :, low + 2 - kh : high + 2 - kh] += dot_t(left, right).reshape(frames, high - low, width, part)

    for fetch in weights[:2]:
        fetch.wait()

    @pl.when(first)
    def _():
        local.wait()
        all_taps(2, 0, 1)
        all_taps(0, rows - 1, rows)
        for t in late:
            send_edges(t)
        all_taps(2, 1, rows)
        all_taps(0, 0, rows - 1)
        weights[2].wait()
        all_taps(1, 0, rows)

    @pl.when(here.has_prev)
    def _():
        for kh in order[:2]:
            taps(kh, *fresh)
        weights[2].wait()
        taps(order[2], *fresh)
        for f in late:
            across[f].wait_recv()
            share[f].start()
            share[f].wait_recv()
            for kh in order[:2]:
                taps(kh, *uses((f,)))
            send_edges(f)
        taps(order[2], *stale)

    later()
    for ok, copy, k, row in ((here.up, to_down, 0, 1), (here.down, to_up, 1, rows)):

        @pl.when(ok)
        def _():
            for t in late:
                copy[t].wait_recv()
                got_edge = edge_in[k, t].astype(F32)
                for at in (0, 1):
                    block = slice(at * width // 2, (at + 1) * width // 2)
                    acc[1, t, row, block] += got_edge[:, at * part : (at + 1) * part]

    def finish(t):
        for r in range(rows):
            v = joined(t, 1 + r)
            seg[t, r] = jnp.concatenate([v, v], axis=1).astype(BF)

    finish(1 - c)
    swap.start()
    finish(c)
    lower = lax.broadcasted_iota(jnp.int32, (width, ch), 1) < part
    kept = lower == (c == 0)
    swap.wait_recv()
    for r in range(rows):
        every[z * rows + r] = jnp.where(kept, seg[c, r].astype(F32), got[r].astype(F32)).astype(BF)

    def drain():
        swap.wait_send()
        for f in late:
            pl.when(here.has_prev)(lambda: share[f].wait_send())
            pl.when(here.has_next)(lambda: across[f].wait_send())
        for t in range(frames):
            pl.when(here.up)(lambda: to_up[t].wait_send())
            pl.when(here.down)(lambda: to_down[t].wait_send())

    return drain


def attn_part(
    here, later, gain_attn, wqk, wvo, every, own, across,
    keys, q_own, q_edge, y_own, y_edge, top_own, top_edge, sum_own, sum_edge, send, recv,
):
    total, width, ch = every.shape
    z, chips = here.z, here.rows
    rows = total // chips
    mine = z * rows
    gain = gain_attn[...].reshape(1, ch)
    sides = ((-1, here.down, {"rows": z + 1}), (1, here.up, {"rows": z - 1}))

    def copy(row, side):
        return remote(every.at[row], every.at[row], send.at[row, side], recv.at[row], sides[side][2])

    def turn(side, r):
        return r if side else rows - 1 - r

    for r in range(rows):
        for side, (_, ok, _) in enumerate(sides):
            pl.when(ok)(lambda: copy(mine + turn(side, r), side).start())

    def norm_rows(src):
        for r in range(rows):
            keys[src * rows + r] = normed(every[src * rows + r].astype(F32), gain).astype(BF)

    def update(chunk, src, count=1):
        q, y, top, total = chunk
        some = keys[pl.ds(src * rows, count * rows)].reshape(count * rows * width, ch)
        s = dot_t(q[...], some)
        high = jnp.maximum(top[...], jnp.max(s, axis=-1, keepdims=True))
        p = jnp.exp2(s - high)
        fade = jnp.exp2(top[...] - high)
        top[...] = high
        total[...] = total[...] * fade + jnp.sum(p, axis=-1, keepdims=True)
        y[...] = y[...] * fade + dot(p.astype(BF), some)

    inner = (q_own, y_own, top_own, sum_own)
    outer = (q_edge, y_edge, top_edge, sum_edge)
    for _, y, top, count in (inner, outer):
        y[...] = jnp.zeros(y.shape, F32)
        top[...] = jnp.full(top.shape, -jnp.inf, F32)
        count[...] = jnp.zeros(count.shape, F32)
    norm_rows(z)
    q_own[...] = dot(keys[pl.ds(mine, rows)].reshape(rows * width, ch), wqk[...]).astype(BF)
    later()
    edges = ((here.up, mine - 1, 0), (here.down, mine + rows, 1))

    def spots(k):
        return ((z - k, z - k >= 0), (z + k, z + k < chips))

    def outer_update(k):
        for src, valid in spots(k):
            pl.when(valid)(lambda: update(outer, src))

    def outer_start():
        for ok, row, at in edges:
            part = pl.ds(at * width, width)

            @pl.when(ok)
            def _():
                q_edge[part, :] = dot(keys[row], wqk[...]).astype(BF)

            @pl.when(jnp.logical_not(ok))
            def _():
                q_edge[part, :] = jnp.zeros((width, ch), BF)

        nearby(outer)

    def nearby(chunk):
        inside = here.up & here.down
        if chips > 2:
            pl.when(inside)(lambda: update(chunk, z - 1, 3))
        if chips > 1:
            pl.when(jnp.logical_not(inside))(lambda: update(chunk, z - here.up.astype(jnp.int32), 2))
        else:
            update(chunk, z)

    def land(k, r):
        for side, (src, valid) in enumerate(spots(k)):

            @pl.when(valid)
            def _():
                row = src * rows + turn(side, r)
                copy(row, side).wait_recv()
                pl.when(sides[side][1])(lambda: copy(row, side).start())

    def hop(k, _):
        land(k, 0)
        pl.when(k == 2)(outer_start)
        pl.when(k > 2)(lambda: outer_update(k - 1))
        for r in range(1, rows):
            land(k, r)
        for src, valid in spots(k):

            @pl.when(valid)
            def _():
                norm_rows(src)
                pl.when(k > 1)(lambda: update(inner, src))

        pl.when(k == 1)(lambda: nearby(inner))
        return 0

    lax.fori_loop(1, chips, hop, 0)
    if chips < 2:
        nearby(inner)

    def close(chunk):
        _, y, _, count = chunk
        return dot((y[...] / count[...]).astype(BF), wvo[...])

    o = close(inner)
    for r in range(rows):
        own[1 + r] = (every[mine + r].astype(F32) + o[r * width : (r + 1) * width]).astype(BF)
    for back in (0, 1):

        @pl.when(here.has_next & (here.c == back))
        def _():
            for copy_row in across[:: 1 - 2 * back]:
                copy_row.start()

    if chips < 3:
        outer_start()
    else:
        outer_update(chips - 1)
    o = close(outer)
    for ok, row, at in edges:
        slot = at * (rows + 1)

        @pl.when(ok)
        def _():
            own[slot] = (every[row].astype(F32) + o[at * width : (at + 1) * width]).astype(BF)

        @pl.when(jnp.logical_not(ok))
        def _():
            own[slot] = jnp.zeros((width, ch), BF)

    def drain():
        def each(k, _):
            for side, (src, valid) in enumerate(spots(k)):

                @pl.when(valid & sides[side][1])
                def _():
                    for r in range(rows):
                        copy(src * rows + r, side).wait_send()

            return 0

        lax.fori_loop(0, chips, each, 0)

    return drain


def last_part(
    here, own, cache, gain, wup, wlow_hbm, out, across,
    x, acc, wlow, prior, chalo, wfull, wmix, wtap, grid, upper, flat, made,
    os, ps, pr, cs, cr, ws, wr, ls, fs, es, er, us, ur,
):
    frames = cache.shape[0]
    height, width, ch = own.shape
    c, z = here.c, here.z
    tall = cache.shape[1]
    low = cache.shape[2]
    wide = cache.shape[3]
    two = 2 * low
    part = wup.shape[2]
    first = jnp.logical_not(here.has_prev)
    fetch = pltpu.make_async_copy(wlow_hbm, wlow, fs)
    fetch.start()
    local = pltpu.make_async_copy(wup, wfull.at[c], ls)
    local.start()
    relays = (
        (0, here.up, remote(prior.at[1], prior.at[height - 1], ps.at[0], pr.at[0], {"rows": z - 1})),
        (height - 3, here.down, remote(prior.at[height - 2], prior.at[0], ps.at[1], pr.at[1], {"rows": z + 1})),
    )
    to_up = remote(cache.at[:, 0], chalo.at[1], cs.at[0], cr.at[0], {"rows": z - 1})
    to_down = remote(cache.at[:, tall - 1], chalo.at[0], cs.at[1], cr.at[1], {"rows": z + 1})
    weights = remote(wup, wfull.at[c], ws, wr, {"chan": 1 - c})

    weights.start()
    yield
    for edge, inside in ((0, here.up), (own.shape[0] - 1, here.down)):

        @pl.when(jnp.logical_not(inside))
        def _():
            prior[edge] = jnp.zeros(own.shape[1:], BF)

    taps_t, taps_h = wlow.shape[:2]
    fetch.wait()

    def lay(i, _):
        kt, kh = i // taps_h, i % taps_h
        tap = [wlow[kt, kh, k * low : (k + 1) * low] for k in range(3)]
        none = jnp.zeros((low, part), BF)
        blocks = ((tap[1], tap[0]), (tap[2], tap[1]), (none, tap[2]), (tap[0], none))
        for at, (even, odd) in enumerate(blocks):
            wtap[kt, kh, at * low : (at + 1) * low, :] = jnp.concatenate([even, odd], axis=1)
        return 0

    lax.fori_loop(0, taps_t * taps_h, lay, 0)

    local.wait()
    weights.wait_recv()
    groups = (((0, 1), (2,)), ((0,), (1, 2)))
    columns = ((1, 2), (0, 1), (0,), (2,))
    for parity, slots in enumerate(groups):
        for slot, khs in enumerate(slots):
            for half in (0, 1):
                by_kw = [sum(wfull[half, kh, kw].astype(F32) for kh in khs) for kw in range(3)]
                for at, kws in enumerate(columns):
                    start = at * low + half * part
                    wmix[parity, start : start + part, slot * ch : (slot + 1) * ch] = sum(by_kw[kw] for kw in kws).astype(BF)

    yield
    pl.when(first & here.up)(lambda: to_up.start())
    pl.when(first & here.down)(lambda: to_down.start())

    gains = gain[...].reshape(1, low)
    gains = jnp.concatenate([gains, gains], axis=1)
    lanes = 128
    starts = range(0, two, lanes)
    lane = lax.broadcasted_iota(jnp.int32, (width, lanes), 1)
    col = lax.broadcasted_iota(jnp.int32, (width, lanes), 0)

    def choose(start, first, last):
        if start + lanes <= low:
            return first()
        if start >= low:
            return last()
        return jnp.where(lane + start < low, first(), last())

    def prev(v):
        return jnp.where(col == 0, 0.0, pltpu.roll(v, 1, 0))

    def following(v):
        return jnp.where(col == width - 1, 0.0, pltpu.roll(v, width - 1, 0))

    def cut_up(v):
        return [v[:, a : a + lanes] for a in starts]

    def beside(slot, row, pieces):
        for a, v in zip(starts, pieces):
            x[slot, tall + 2 + row, :, a : a + lanes] = choose(a, lambda: following(v), lambda: prev(v)).astype(BF)

    def put(slot, row, pieces):
        for a, v in zip(starts, pieces):
            x[slot, row, :, a : a + lanes] = v.astype(BF)
        beside(slot, row, pieces)

    def row_copy(slot, at, r):
        piece = x.at[slot, r]
        return remote(piece, piece, es.at[at, r], er.at[at, r], {"chan": 1 - c})

    def upper_copy(f, r):
        return remote(upper.at[f, r], upper.at[f, r], us.at[r], ur.at[r], {"chan": 1 - c})

    def raise_frame(tile, at):
        slot = at * frames + c
        n = height - 1
        pairs = jnp.concatenate([tile[0:n], tile[1 : n + 1]], axis=2).reshape(n * width, 2 * ch)
        for parity in (0, 1):
            grid[parity] = dot_t(pairs, wmix[parity]).reshape(n, width, 2 * two)
        for r in range(tall + 2):
            same, cross = grid[r % 2, r // 2, :, :two], grid[r % 2, r // 2, :, two:]
            vs = [
                (v + choose(a, lambda: prev(u), lambda: following(u))).astype(BF)
                for a, v, u in zip(starts, cut_up(same), cut_up(cross))
            ]
            if at and 0 < r <= tall:
                for a, v in zip(starts, vs):
                    upper[c, r - 1, :, a : a + lanes] = v
                upper_copy(c, r - 1).start()
            vs = [v.astype(F32) for v in vs]
            zero = jnp.zeros((width, lanes), F32)
            mean_even = sum(choose(a, lambda: v * v, lambda: zero) for a, v in zip(starts, vs) if a < low)
            mean_odd = sum(choose(a, lambda: zero, lambda: v * v) for a, v in zip(starts, vs) if a + lanes > low)
            by_even, by_odd = (
                lax.rsqrt(jnp.sum(m, axis=-1, keepdims=True) / low + 1e-06) for m in (mean_even, mean_odd)
            )
            vs = [
                silu(v * choose(a, lambda: by_even, lambda: by_odd) * gains[:, a : a + lanes]) for a, v in zip(starts, vs)
            ]
            if r == 0:
                vs = [jnp.where(here.up, v, 0.0) for v in vs]
            if r == tall + 1:
                vs = [jnp.where(here.down, v, 0.0) for v in vs]
            put(slot, r, vs)
            row_copy(slot, at, r).start()

    def land(at):
        other = at * frames + 1 - c
        for r in range(tall + 2):
            row_copy(other, at, r).wait_recv()
            beside(other, r, cut_up(x[other, r].astype(F32)))

    raise_frame(own, 1)

    @pl.when(here.has_prev)
    def _():
        for back in (0, 1):

            @pl.when(c == back)
            def _():
                for r in range(len(across))[:: 1 - 2 * back]:
                    across[r].wait_recv()
                    for at, ok, relay in relays:
                        if at == r:
                            pl.when(ok)(lambda: relay.start())

    n = 2 * part
    pick = picker(two, n, lambda k, j: k == jnp.where(j < part, j, j - part + low) + c * part)
    for r in range(tall):
        upper_copy(1 - c, r).wait_recv()
    acc[...] = dot(upper[...].reshape(-1, two), pick)

    def run_taps(at, pair, before):
        def each(i, _):
            turned = c * (2 if at else 1)
            e = (i + turned) % taps_t
            t, kt = pair(e)
            own_first = 1 + (1 - c if at else c)
            pl.when(before & (i == own_first))(lambda: land(at))
            block = pl.ds(pl.multiple_of(t * tall * width, tall * width), tall * width)

            def tap(kh, _):
                v = jnp.concatenate([x[t + kt, pl.ds(k * (tall + 2) + kh, tall)] for k in (0, 1)], axis=2)
                acc[block, :] += dot(v.reshape(tall * width, 2 * two), wtap[kt, kh])
                return 0

            for kh in range(taps_h):
                tap(kh, 0)
            return 0

        lax.fori_loop(0, taps_t, each, 0)

    run_taps(1, lambda e: ((e + 1) // 2, 2 - e % 2), c >= 0)

    @pl.when(here.has_prev)
    def _():
        pl.when(here.down)(lambda: relays[0][2].wait_recv())
        pl.when(here.up)(lambda: relays[1][2].wait_recv())
        raise_frame(prior, 0)

    spots = [picker(width, wide, lambda k, n: n == 2 * k + p) for p in (0, 1)]

    def take(slot, row, flipped):
        put(slot, row, cut_up(jnp.concatenate([dot_t(spot, flipped) for spot in spots], axis=1)))

    @pl.when(first)
    def _():
        def each(i, _):
            take(i // tall, 1 + i % tall, cache[i // tall, i % tall])
            return 0

        lax.fori_loop(0, frames * tall, each, 0)

    for row, inside, k, copy in ((0, here.up, 0, to_down), (tall + 1, here.down, 1, to_up)):

        @pl.when(first & inside)
        def _():
            copy.wait_recv()
            for f in range(frames):
                take(f, row, chalo[k, f])

        @pl.when(first & jnp.logical_not(inside))
        def _():
            for f in range(frames):
                put(f, row, cut_up(jnp.zeros((width, two), F32)))

    run_taps(0, lambda e: (e // 2, e % 2), here.has_prev)

    def turn(i, _):
        done = acc[pl.ds(pl.multiple_of(i * width, width), width), :].astype(BF).T
        for p in (0, 1):
            flat[p, i] = done[p * part : (p + 1) * part]
        return 0

    lax.fori_loop(0, frames * tall, turn, 0)
    for f in range(frames):
        sides = [flat[p, f * tall : (f + 1) * tall].reshape(tall * part, width) for p in (0, 1)]
        made[f] = (dot(sides[0], spots[0]) + dot(sides[1], spots[1])).astype(BF).reshape(tall, part, wide)
        pltpu.make_async_copy(made.at[f], out.at[f], os.at[f]).start()
    for f in range(frames):
        pltpu.make_async_copy(made.at[f], out.at[f], os.at[f]).wait()
    weights.wait_send()
    for r in range(tall):
        upper_copy(c, r).wait_send()
    for r in range(tall + 2):
        row_copy(frames + c, 1, r).wait_send()

    @pl.when(here.has_prev)
    def _():
        for _, ok, relay in relays:
            pl.when(ok)(lambda: relay.wait_send())
        for r in range(tall + 2):
            row_copy(c, 0, r).wait_send()

    for copy in across:
        pl.when(here.has_next)(lambda: copy.wait_send())
    pl.when(first & here.up)(lambda: to_up.wait_send())
    pl.when(first & here.down)(lambda: to_down.wait_send())


def whole_kernel(counts, *refs):
    groups = []
    for count in counts:
        groups.append(refs[:count])
        refs = refs[count:]
    ins, (out,), shared, first, attn, last = groups
    latent, cache_mid, cache_low, gain_mid, gain_attn, gain_low, conv_mid, attn_qkv, attn_proj, conv_up, conv_low = ins
    every, own, prior, wqkv, wproj, wqk, wvo, low_cache, sems, xs, xr = shared
    fetches = [
        pltpu.make_async_copy(src, dst, sems.at[i])
        for i, (src, dst) in enumerate(((attn_qkv, wqkv), (attn_proj, wproj), (cache_low, low_cache)))
    ]
    here = Place()
    rows, ch = own.shape[0] - 2, own.shape[2]
    across = [
        remote(own.at[1 + r], prior.at[1 + r], xs.at[r], xr.at[r], {"segment": here.s + 1}) for r in range(rows)
    ]
    tail = last_part(here, own, low_cache, gain_low, conv_up, conv_low, out, across, *last[:2], last[2], prior, *last[3:])

    def begun():
        for fetch in fetches:
            fetch.start()
        next(tail)

    def fold():
        for fetch in fetches:
            fetch.wait()
        wqk[...] = (dot_t(wqkv[:, :ch], wqkv[:, ch : 2 * ch]) * (math.log2(math.e) / math.sqrt(ch))).astype(BF)
        wvo[...] = dot(wqkv[:, 2 * ch :], wproj[...]).astype(BF)

    drains = [first_part(here, latent, cache_mid, gain_mid, conv_mid, every, begun, fold, *first)]
    drains.append(attn_part(here, lambda: next(tail), gain_attn, wqk, wvo, every, own, across, *attn))
    next(tail, None)
    for drain in drains:
        drain()


def call(kernel, number, outs, scratch, *args, far=()):
    return pl.pallas_call(
        kernel,
        out_shape=outs,
        in_specs=[pl.BlockSpec(memory_space=pl.ANY if i in far else pltpu.VMEM) for i in range(len(args))],
        out_specs=pl.BlockSpec(memory_space=pl.ANY),
        scratch_shapes=scratch,
        compiler_params=pltpu.CompilerParams(
            collective_id=number, has_side_effects=True, vmem_limit_bytes=59500000
        ),
    )(*args)


def body(
    latent, cache_mid, cache_low, gain_mid, gain_attn, gain_low, conv_mid, attn_qkv, attn_proj, conv_up, conv_low
):
    frames, rows, width, ch = latent.shape
    part = conv_mid.shape[-1]
    dma, one = pltpu.SemaphoreType.DMA, pltpu.SemaphoreType.DMA(())
    taps_t, taps_h, taps_w = conv_mid.shape[:3]
    total = rows * lax.axis_size("rows")
    cache_t = jnp.swapaxes(cache_low, 2, 3)
    tile = pltpu.VMEM((rows + 2, width, ch), BF)
    shared = [
        pltpu.VMEM((total, width, ch), BF), tile, tile,
        pltpu.VMEM(attn_qkv.shape, BF), pltpu.VMEM(attn_proj.shape, BF),
        pltpu.VMEM((ch, ch), BF), pltpu.VMEM((ch, ch), BF), pltpu.VMEM(cache_t.shape, BF),
        dma((3,)), dma((rows,)), dma((rows,)),
    ]
    first = [
        pltpu.VMEM(latent.shape, BF),
        pltpu.VMEM((taps_t - 1 + frames, rows, width, ch), BF),
        pltpu.VMEM((taps_t, taps_h, taps_w, part, ch), BF),
        pltpu.VMEM((taps_w, frames, rows + 2, width, part), F32),
        pltpu.VMEM((2, frames, width // 2, 2 * part), BF),
        pltpu.VMEM((2, frames, width // 2, 2 * part), BF),
        pltpu.VMEM((frames, rows, width, ch), BF),
        pltpu.VMEM((rows, width, ch), BF),
        dma((2, frames)), dma((2, frames)), *(dma((taps_t - 1,)) for _ in range(4)), one, one, dma((2,)), dma((taps_h,)),
    ]
    sizes = (rows * width, 2 * width)
    attn = [
        pltpu.VMEM((total, width, ch), BF),
        *(pltpu.VMEM((n, ch), BF) for n in sizes),
        *(pltpu.VMEM((n, ch), F32) for n in sizes),
        *(pltpu.VMEM((n, 1), F32) for n in sizes),
        *(pltpu.VMEM((n, 1), F32) for n in sizes),
        dma((total, 2)),
        dma((total,)),
    ]
    _, tall, wide, low = cache_low.shape
    cut = conv_low.shape[-1]
    two = 2 * low
    taps_t, taps_h, taps_w = conv_low.shape[:3]
    last = [
        pltpu.VMEM((2 * frames, 2 * (tall + 2), width, two), BF),
        pltpu.VMEM((frames * tall * width, 2 * cut), F32),
        pltpu.VMEM((taps_t, taps_h, taps_w * low, cut), BF),
        pltpu.VMEM((2, frames, low, wide), BF),
        pltpu.VMEM((2, 3, 3, cut, ch), BF),
        pltpu.VMEM((2, 2 * two, 2 * ch), BF),
        pltpu.VMEM((taps_t, taps_h, 2 * two, 2 * cut), BF),
        pltpu.VMEM((2, rows + 1, width, 2 * two), F32),
        pltpu.VMEM((frames, tall, width, two), BF),
        pltpu.VMEM((2, frames * tall, cut, width), BF),
        pltpu.VMEM((frames, tall, cut, wide), BF),
        dma((frames,)), dma((2,)), dma((2,)), dma((2,)), dma((2,)), one, one, one, one,
        dma((2, tall + 2)), dma((2, tall + 2)), dma((tall,)), dma((tall,)),
    ]
    args = (
        latent, cache_mid, cache_t, gain_mid, gain_attn, gain_low, jnp.swapaxes(conv_mid, 3, 4), attn_qkv, attn_proj,
        jnp.swapaxes(conv_up, 2, 3), conv_low.reshape(taps_t, taps_h, taps_w * low, cut),
    )
    counts = (len(args), 1, len(shared), len(first), len(attn), len(last))
    decoded = call(
        functools.partial(whole_kernel, counts),
        0,
        pltpu.VMEM((frames, tall, cut, wide), BF),
        shared + first + attn + last,
        *args,
        far=(0, 1, 2, 6, 7, 8, 9, 10),
    )
    return jnp.swapaxes(decoded, 2, 3)


def solution(mesh):
    placed = (
        P(("groups", "segment"), "rows", None, None),
        P("groups", "rows", None, None),
        P("groups", "rows", None, None),
        P(),
        P(),
        P(),
        P(None, None, None, None, "chan"),
        P(),
        P(),
        P(None, None, None, "chan"),
        P(None, None, None, None, "chan"),
    )
    return jax.shard_map(
        body,
        mesh=mesh,
        in_specs=placed,
        out_specs=P(("groups", "segment"), "rows", None, "chan"),
        check_vma=False,
    )
```

```python
import functools
import math

import jax
import jax.numpy as jnp
from jax import lax
from jax.experimental import pallas as pl
from jax.experimental.pallas import tpu as pltpu
from jax.sharding import PartitionSpec as P

MESH = pl.DeviceIdType.MESH
BF = jnp.bfloat16
F32 = jnp.float32


class Place:
    def __init__(self):
        self.rows, self.segs = lax.axis_size("rows"), lax.axis_size("segment")
        self.z, self.s, self.c = (lax.axis_index(a) for a in ("rows", "segment", "chan"))
        self.up, self.down = self.z > 0, self.z < self.rows - 1
        self.has_next, self.has_prev = self.s < self.segs - 1, self.s > 0

    def greet(self):
        barrier = pltpu.get_barrier_semaphore()
        n = jnp.int32(1)
        pl.semaphore_signal(barrier, inc=1, device_id={"chan": 1 - self.c}, device_id_type=MESH)
        for ok, target in (
            (self.up, {"rows": self.z - 1}),
            (self.down, {"rows": self.z + 1}),
            (self.has_next, {"segment": self.s + 1}),
            (self.has_prev, {"segment": self.s - 1}),
        ):

            @pl.when(ok)
            def _():
                pl.semaphore_signal(barrier, inc=1, device_id=target, device_id_type=MESH)

            n = n + ok.astype(jnp.int32)
        return lambda: pl.semaphore_wait(barrier, n)


def remote(src, dst, send, recv, target):
    return pltpu.make_async_remote_copy(
        src_ref=src, dst_ref=dst, send_sem=send, recv_sem=recv, device_id=target, device_id_type=MESH
    )


def normed(v, gain):
    return v * lax.rsqrt(jnp.mean(v * v, axis=-1, keepdims=True) + 1e-06) * gain


def silu(v):
    return 0.5 * v * (1.0 + jnp.tanh(0.5 * v))


def dot(a, b):
    return jnp.dot(a, b, preferred_element_type=F32)


def dot_t(a, b):
    return lax.dot_general(a, b, (((1,), (1,)), ((), ())), preferred_element_type=F32)


def picker(rows, cols, hit):
    k = lax.broadcasted_iota(jnp.int32, (rows, cols), 0)
    n = lax.broadcasted_iota(jnp.int32, (rows, cols), 1)
    return jnp.where(hit(k, n), 1.0, 0.0).astype(BF)


def first_part(
    here, latent_hbm, cache_hbm, gain_mid, w_hbm, every, begun, later,
    latent, xa, w, acc, edge_out, edge_in, seg, got, es, er, xs, xr, ps, pr, gs, gr, ls, wsem,
):
    frames, rows, width, ch = latent.shape
    taps_t, taps_h, taps_w, part = w.shape[:4]
    before = taps_t - 1
    c, z = here.c, here.z
    first = jnp.logical_not(here.has_prev)
    order = (2, 0, 1)
    met = here.greet()
    own = pltpu.make_async_copy(latent_hbm, latent, ls.at[0])
    local = pltpu.make_async_copy(cache_hbm, xa.at[pl.ds(0, before)], ls.at[1])
    weights = [pltpu.make_async_copy(w_hbm.at[:, kh], w.at[:, kh], wsem.at[kh]) for kh in order]
    own.start()
    pl.when(first)(lambda: local.start())
    for fetch in weights:
        fetch.start()
    acc[...] = jnp.zeros(acc.shape, F32)
    half = rows // 2

    def piece(f):
        return xa.at[f, pl.ds(c * half, half)]

    across = [remote(piece(before + f), piece(f), xs.at[f], xr.at[f], {"segment": here.s + 1}) for f in range(before)]
    share = [remote(piece(f), piece(f), ps.at[f], pr.at[f], {"chan": 1 - c}) for f in range(before)]
    to_up, to_down = (
        [remote(edge_out.at[k, t], edge_in.at[1 - k, t], es.at[k, t], er.at[1 - k, t], {"rows": z + side}) for t in range(frames)]
        for k, side in ((0, -1), (1, 1))
    )
    swap = remote(seg.at[1 - c], got, gs, gr, {"chan": 1 - c})

    own.wait()
    gain = gain_mid[...].reshape(1, ch)

    def fill(f, side):
        for r in range(half):
            row = side * half + r
            xa[before + f, row] = silu(normed(latent[f, row].astype(F32), gain)).astype(BF)

    late = tuple(range(before))[::-1]
    fill(late[0], c)
    met()
    for f in late:
        if f != late[0]:
            fill(f, c)
        pl.when(here.has_next)(lambda: across[f].start())
    begun()
    for f in range(frames):
        fill(f, 1 - c)
    pick = picker(ch, part, lambda k, n: k == n + c * part)
    for t in range(frames):
        acc[1, t, 1 : 1 + rows] = dot(latent[t].reshape(rows * width, ch), pick).reshape(rows, width, part)

    def taps(kh, *uses):
        for t, some in uses:
            left = jnp.concatenate([xa[t + kt].reshape(rows * width, ch) for kt in some], axis=1)
            for kw in range(taps_w):
                right = jnp.concatenate([w[kt, kh, kw] for kt in some], axis=1)
                acc[kw, t, 2 - kh : 2 - kh + rows] += dot_t(left, right).reshape(rows, width, part)

    def uses(frames_in):
        return [(t, some) for t in range(frames) if (some := [kt for kt in range(taps_t) if t + kt in frames_in])]

    fresh = uses(range(before, before + frames))
    stale = uses(range(before))
    col = lax.broadcasted_iota(jnp.int32, (width, part), 0)

    def joined(t, row):
        left = jnp.where(col == 0, 0.0, pltpu.roll(acc[0, t, row], 1, 0))
        right = jnp.where(col == width - 1, 0.0, pltpu.roll(acc[2, t, row], width - 1, 0))
        return acc[1, t, row] + left + right

    def send_edges(t):
        for k, row in enumerate((0, rows + 1)):
            v = joined(t, row)
            edge_out[k, t] = jnp.concatenate([v[: width // 2], v[width // 2 :]], axis=1).astype(BF)
        pl.when(here.up)(lambda: to_up[t].start())
        pl.when(here.down)(lambda: to_down[t].start())

    def all_taps(kh, low, high):
        n = frames * (high - low) * width
        left = jnp.concatenate([xa[kt : kt + frames, low:high].reshape(n, ch) for kt in range(taps_t)], axis=1)

        for kw in range(taps_w):
            right = jnp.concatenate([w[kt, kh, kw] for kt in range(taps_t)], axis=1)
            acc[kw, :, low + 2 - kh : high + 2 - kh] += dot_t(left, right).reshape(frames, high - low, width, part)

    for fetch in weights[:2]:
        fetch.wait()

    @pl.when(first)
    def _():
        local.wait()
        all_taps(2, 0, 1)
        all_taps(0, rows - 1, rows)
        for t in late:
            send_edges(t)
        all_taps(2, 1, rows)
        all_taps(0, 0, rows - 1)
        weights[2].wait()
        all_taps(1, 0, rows)

    @pl.when(here.has_prev)
    def _():
        for kh in order[:2]:
            taps(kh, *fresh)
        weights[2].wait()
        taps(order[2], *fresh)
        for f in late:
            across[f].wait_recv()
            share[f].start()
            share[f].wait_recv()
            for kh in order[:2]:
                taps(kh, *uses((f,)))
            send_edges(f)
        taps(order[2], *stale)

    later()
    for ok, copy, k, row in ((here.up, to_down, 0, 1), (here.down, to_up, 1, rows)):

        @pl.when(ok)
        def _():
            for t in late:
                copy[t].wait_recv()
                got_edge = edge_in[k, t].astype(F32)
                for at in (0, 1):
                    block = slice(at * width // 2, (at + 1) * width // 2)
                    acc[1, t, row, block] += got_edge[:, at * part : (at + 1) * part]

    def finish(t):
        for r in range(rows):
            v = joined(t, 1 + r)
            seg[t, r] = jnp.concatenate([v, v], axis=1).astype(BF)

    finish(1 - c)
    swap.start()
    finish(c)
    lower = lax.broadcasted_iota(jnp.int32, (width, ch), 1) < part
    kept = lower == (c == 0)
    swap.wait_recv()
    for r in range(rows):
        every[z * rows + r] = jnp.where(kept, seg[c, r].astype(F32), got[r].astype(F32)).astype(BF)

    def drain():
        swap.wait_send()
        for f in late:
            pl.when(here.has_prev)(lambda: share[f].wait_send())
            pl.when(here.has_next)(lambda: across[f].wait_send())
        for t in range(frames):
            pl.when(here.up)(lambda: to_up[t].wait_send())
            pl.when(here.down)(lambda: to_down[t].wait_send())

    return drain


def attn_part(
    here, later, gain_attn, wqk, wvo, every, own, across,
    keys, q_own, q_edge, y_own, y_edge, top_own, top_edge, sum_own, sum_edge, send, recv,
):
    total, width, ch = every.shape
    z, chips = here.z, here.rows
    rows = total // chips
    mine = z * rows
    gain = gain_attn[...].reshape(1, ch)
    sides = ((-1, here.down, {"rows": z + 1}), (1, here.up, {"rows": z - 1}))

    def copy(row, side):
        return remote(every.at[row], every.at[row], send.at[row, side], recv.at[row], sides[side][2])

    def turn(side, r):
        return r if side else rows - 1 - r

    for r in range(rows):
        for side, (_, ok, _) in enumerate(sides):
            pl.when(ok)(lambda: copy(mine + turn(side, r), side).start())

    def norm_rows(src):
        for r in range(rows):
            keys[src * rows + r] = normed(every[src * rows + r].astype(F32), gain).astype(BF)

    def update(chunk, src, count=1):
        q, y, top, total = chunk
        some = keys[pl.ds(src * rows, count * rows)].reshape(count * rows * width, ch)
        s = dot_t(q[...], some)
        high = jnp.maximum(top[...], jnp.max(s, axis=-1, keepdims=True))
        p = jnp.exp2(s - high)
        fade = jnp.exp2(top[...] - high)
        top[...] = high
        total[...] = total[...] * fade + jnp.sum(p, axis=-1, keepdims=True)
        y[...] = y[...] * fade + dot(p.astype(BF), some)

    inner = (q_own, y_own, top_own, sum_own)
    outer = (q_edge, y_edge, top_edge, sum_edge)
    for _, y, top, count in (inner, outer):
        y[...] = jnp.zeros(y.shape, F32)
        top[...] = jnp.full(top.shape, -jnp.inf, F32)
        count[...] = jnp.zeros(count.shape, F32)
    norm_rows(z)
    q_own[...] = dot(keys[pl.ds(mine, rows)].reshape(rows * width, ch), wqk[...]).astype(BF)
    later()
    edges = ((here.up, mine - 1, 0), (here.down, mine + rows, 1))

    def spots(k):
        return ((z - k, z - k >= 0), (z + k, z + k < chips))

    def outer_update(k):
        for src, valid in spots(k):
            pl.when(valid)(lambda: update(outer, src))

    def outer_start():
        for ok, row, at in edges:
            part = pl.ds(at * width, width)

            @pl.when(ok)
            def _():
                q_edge[part, :] = dot(keys[row], wqk[...]).astype(BF)

            @pl.when(jnp.logical_not(ok))
            def _():
                q_edge[part, :] = jnp.zeros((width, ch), BF)

        nearby(outer)

    def nearby(chunk):
        inside = here.up & here.down
        if chips > 2:
            pl.when(inside)(lambda: update(chunk, z - 1, 3))
        if chips > 1:
            pl.when(jnp.logical_not(inside))(lambda: update(chunk, z - here.up.astype(jnp.int32), 2))
        else:
            update(chunk, z)

    def land(k, r):
        for side, (src, valid) in enumerate(spots(k)):

            @pl.when(valid)
            def _():
                row = src * rows + turn(side, r)
                copy(row, side).wait_recv()
                pl.when(sides[side][1])(lambda: copy(row, side).start())

    def hop(k, _):
        land(k, 0)
        pl.when(k == 2)(outer_start)
        pl.when(k > 2)(lambda: outer_update(k - 1))
        for r in range(1, rows):
            land(k, r)
        for src, valid in spots(k):

            @pl.when(valid)
            def _():
                norm_rows(src)
                pl.when(k > 1)(lambda: update(inner, src))

        pl.when(k == 1)(lambda: nearby(inner))
        return 0

    lax.fori_loop(1, chips, hop, 0)
    if chips < 2:
        nearby(inner)

    def close(chunk):
        _, y, _, count = chunk
        return dot((y[...] / count[...]).astype(BF), wvo[...])

    o = close(inner)
    for r in range(rows):
        own[1 + r] = (every[mine + r].astype(F32) + o[r * width : (r + 1) * width]).astype(BF)
    for back in (0, 1):

        @pl.when(here.has_next & (here.c == back))
        def _():
            for copy_row in across[:: 1 - 2 * back]:
                copy_row.start()

    if chips < 3:
        outer_start()
    else:
        outer_update(chips - 1)
    o = close(outer)
    for ok, row, at in edges:
        slot = at * (rows + 1)

        @pl.when(ok)
        def _():
            own[slot] = (every[row].astype(F32) + o[at * width : (at + 1) * width]).astype(BF)

        @pl.when(jnp.logical_not(ok))
        def _():
            own[slot] = jnp.zeros((width, ch), BF)

    def drain():
        def each(k, _):
            for side, (src, valid) in enumerate(spots(k)):

                @pl.when(valid & sides[side][1])
                def _():
                    for r in range(rows):
                        copy(src * rows + r, side).wait_send()

            return 0

        lax.fori_loop(0, chips, each, 0)

    return drain


def last_part(
    here, own, cache, gain, wup, wlow_hbm, out, across,
    x, acc, wlow, prior, chalo, wfull, wmix, wtap, grid, upper, flat,
    ps, pr, cs, cr, ws, wr, ls, fs, es, er, us, ur,
):
    frames = cache.shape[0]
    height, width, ch = own.shape
    c, z = here.c, here.z
    tall = cache.shape[1]
    low = cache.shape[2]
    wide = cache.shape[3]
    two = 2 * low
    part = wup.shape[2]
    first = jnp.logical_not(here.has_prev)
    fetch = pltpu.make_async_copy(wlow_hbm, wlow, fs)
    fetch.start()
    local = pltpu.make_async_copy(wup, wfull.at[c], ls)
    local.start()
    relays = (
        (0, here.up, remote(prior.at[1], prior.at[height - 1], ps.at[0], pr.at[0], {"rows": z - 1})),
        (height - 3, here.down, remote(prior.at[height - 2], prior.at[0], ps.at[1], pr.at[1], {"rows": z + 1})),
    )
    to_up = remote(cache.at[:, 0], chalo.at[1], cs.at[0], cr.at[0], {"rows": z - 1})
    to_down = remote(cache.at[:, tall - 1], chalo.at[0], cs.at[1], cr.at[1], {"rows": z + 1})
    weights = remote(wup, wfull.at[c], ws, wr, {"chan": 1 - c})

    weights.start()
    yield
    for edge, inside in ((0, here.up), (own.shape[0] - 1, here.down)):

        @pl.when(jnp.logical_not(inside))
        def _():
            prior[edge] = jnp.zeros(own.shape[1:], BF)

    taps_t, taps_h = wlow.shape[:2]
    fetch.wait()

    def lay(i, _):
        kt, kh = i // taps_h, i % taps_h
        tap = [wlow[kt, kh, k * low : (k + 1) * low] for k in range(3)]
        none = jnp.zeros((low, part), BF)
        blocks = ((tap[1], tap[0]), (tap[2], tap[1]), (none, tap[2]), (tap[0], none))
        for at, (even, odd) in enumerate(blocks):
            wtap[kt, kh, at * low : (at + 1) * low, :] = jnp.concatenate([even, odd], axis=1)
        return 0

    lax.fori_loop(0, taps_t * taps_h, lay, 0)

    local.wait()
    weights.wait_recv()
    groups = (((0, 1), (2,)), ((0,), (1, 2)))
    columns = ((1, 2), (0, 1), (0,), (2,))
    for parity, slots in enumerate(groups):
        for slot, khs in enumerate(slots):
            for half in (0, 1):
                by_kw = [sum(wfull[half, kh, kw].astype(F32) for kh in khs) for kw in range(3)]
                for at, kws in enumerate(columns):
                    start = at * low + half * part
                    wmix[parity, start : start + part, slot * ch : (slot + 1) * ch] = sum(by_kw[kw] for kw in kws).astype(BF)

    yield
    pl.when(first & here.up)(lambda: to_up.start())
    pl.when(first & here.down)(lambda: to_down.start())

    gains = gain[...].reshape(1, low)
    gains = jnp.concatenate([gains, gains], axis=1)
    lanes = 128
    starts = range(0, two, lanes)
    lane = lax.broadcasted_iota(jnp.int32, (width, lanes), 1)
    col = lax.broadcasted_iota(jnp.int32, (width, lanes), 0)

    def choose(start, first, last):
        if start + lanes <= low:
            return first()
        if start >= low:
            return last()
        return jnp.where(lane + start < low, first(), last())

    def prev(v):
        return jnp.where(col == 0, 0.0, pltpu.roll(v, 1, 0))

    def following(v):
        return jnp.where(col == width - 1, 0.0, pltpu.roll(v, width - 1, 0))

    def cut_up(v):
        return [v[:, a : a + lanes] for a in starts]

    def beside(slot, row, pieces):
        for a, v in zip(starts, pieces):
            x[slot, tall + 2 + row, :, a : a + lanes] = choose(a, lambda: following(v), lambda: prev(v)).astype(BF)

    def put(slot, row, pieces):
        for a, v in zip(starts, pieces):
            x[slot, row, :, a : a + lanes] = v.astype(BF)
        beside(slot, row, pieces)

    def row_copy(slot, at, r):
        piece = x.at[slot, r]
        return remote(piece, piece, es.at[at, r], er.at[at, r], {"chan": 1 - c})

    def upper_copy(f, r):
        return remote(upper.at[f, r], upper.at[f, r], us.at[r], ur.at[r], {"chan": 1 - c})

    def raise_frame(tile, at):
        slot = at * frames + c
        n = height - 1
        pairs = jnp.concatenate([tile[0:n], tile[1 : n + 1]], axis=2).reshape(n * width, 2 * ch)
        for parity in (0, 1):
            grid[parity] = dot_t(pairs, wmix[parity]).reshape(n, width, 2 * two)
        for r in range(tall + 2):
            same, cross = grid[r % 2, r // 2, :, :two], grid[r % 2, r // 2, :, two:]
            vs = [
                (v + choose(a, lambda: prev(u), lambda: following(u))).astype(BF)
                for a, v, u in zip(starts, cut_up(same), cut_up(cross))
            ]
            if at and 0 < r <= tall:
                for a, v in zip(starts, vs):
                    upper[c, r - 1, :, a : a + lanes] = v
                upper_copy(c, r - 1).start()
            vs = [v.astype(F32) for v in vs]
            zero = jnp.zeros((width, lanes), F32)
            mean_even = sum(choose(a, lambda: v * v, lambda: zero) for a, v in zip(starts, vs) if a < low)
            mean_odd = sum(choose(a, lambda: zero, lambda: v * v) for a, v in zip(starts, vs) if a + lanes > low)
            by_even, by_odd = (
                lax.rsqrt(jnp.sum(m, axis=-1, keepdims=True) / low + 1e-06) for m in (mean_even, mean_odd)
            )
            vs = [
                silu(v * choose(a, lambda: by_even, lambda: by_odd) * gains[:, a : a + lanes]) for a, v in zip(starts, vs)
            ]
            if r == 0:
                vs = [jnp.where(here.up, v, 0.0) for v in vs]
            if r == tall + 1:
                vs = [jnp.where(here.down, v, 0.0) for v in vs]
            put(slot, r, vs)
            row_copy(slot, at, r).start()

    def land(at):
        other = at * frames + 1 - c
        for r in range(tall + 2):
            row_copy(other, at, r).wait_recv()
            beside(other, r, cut_up(x[other, r].astype(F32)))

    raise_frame(own, 1)

    @pl.when(here.has_prev)
    def _():
        for back in (0, 1):

            @pl.when(c == back)
            def _():
                for r in range(len(across))[:: 1 - 2 * back]:
                    across[r].wait_recv()
                    for at, ok, relay in relays:
                        if at == r:
                            pl.when(ok)(lambda: relay.start())

    n = 2 * part
    pick = picker(two, n, lambda k, j: k == jnp.where(j < part, j, j - part + low) + c * part)
    for r in range(tall):
        upper_copy(1 - c, r).wait_recv()
    acc[...] = dot(upper[...].reshape(-1, two), pick)

    def run_taps(at, pair, before):
        def each(i, _):
            turned = c * (2 if at else 1)
            e = (i + turned) % taps_t
            t, kt = pair(e)
            own_first = 1 + (1 - c if at else c)
            pl.when(before & (i == own_first))(lambda: land(at))
            block = pl.ds(pl.multiple_of(t * tall * width, tall * width), tall * width)

            def tap(kh, _):
                v = jnp.concatenate([x[t + kt, pl.ds(k * (tall + 2) + kh, tall)] for k in (0, 1)], axis=2)
                acc[block, :] += dot(v.reshape(tall * width, 2 * two), wtap[kt, kh])
                return 0

            for kh in range(taps_h):
                tap(kh, 0)
            return 0

        lax.fori_loop(0, taps_t, each, 0)

    run_taps(1, lambda e: ((e + 1) // 2, 2 - e % 2), c >= 0)

    @pl.when(here.has_prev)
    def _():
        pl.when(here.down)(lambda: relays[0][2].wait_recv())
        pl.when(here.up)(lambda: relays[1][2].wait_recv())
        raise_frame(prior, 0)

    spots = [picker(width, wide, lambda k, n: n == 2 * k + p) for p in (0, 1)]

    def take(slot, row, flipped):
        put(slot, row, cut_up(jnp.concatenate([dot_t(spot, flipped) for spot in spots], axis=1)))

    @pl.when(first)
    def _():
        def each(i, _):
            take(i // tall, 1 + i % tall, cache[i // tall, i % tall])
            return 0

        lax.fori_loop(0, frames * tall, each, 0)

    for row, inside, k, copy in ((0, here.up, 0, to_down), (tall + 1, here.down, 1, to_up)):

        @pl.when(first & inside)
        def _():
            copy.wait_recv()
            for f in range(frames):
                take(f, row, chalo[k, f])

        @pl.when(first & jnp.logical_not(inside))
        def _():
            for f in range(frames):
                put(f, row, cut_up(jnp.zeros((width, two), F32)))

    run_taps(0, lambda e: (e // 2, e % 2), here.has_prev)

    def turn(i, _):
        done = acc[pl.ds(pl.multiple_of(i * width, width), width), :].astype(BF).T
        for p in (0, 1):
            flat[p, i] = done[p * part : (p + 1) * part]
        return 0

    lax.fori_loop(0, frames * tall, turn, 0)
    for f in range(frames):
        sides = [flat[p, f * tall : (f + 1) * tall].reshape(tall * part, width) for p in (0, 1)]
        out[f] = (dot(sides[0], spots[0]) + dot(sides[1], spots[1])).astype(BF).reshape(tall, part, wide)
    weights.wait_send()
    for r in range(tall):
        upper_copy(c, r).wait_send()
    for r in range(tall + 2):
        row_copy(frames + c, 1, r).wait_send()

    @pl.when(here.has_prev)
    def _():
        for _, ok, relay in relays:
            pl.when(ok)(lambda: relay.wait_send())
        for r in range(tall + 2):
            row_copy(c, 0, r).wait_send()

    for copy in across:
        pl.when(here.has_next)(lambda: copy.wait_send())
    pl.when(first & here.up)(lambda: to_up.wait_send())
    pl.when(first & here.down)(lambda: to_down.wait_send())


def whole_kernel(counts, *refs):
    groups = []
    for count in counts:
        groups.append(refs[:count])
        refs = refs[count:]
    ins, (out,), shared, first, attn, last = groups
    latent, cache_mid, cache_low, gain_mid, gain_attn, gain_low, conv_mid, attn_qkv, attn_proj, conv_up, conv_low = ins
    every, own, prior, wqkv, wproj, wqk, wvo, low_cache, sems, xs, xr = shared
    fetches = [
        pltpu.make_async_copy(src, dst, sems.at[i])
        for i, (src, dst) in enumerate(((attn_qkv, wqkv), (attn_proj, wproj), (cache_low, low_cache)))
    ]
    here = Place()
    rows, ch = own.shape[0] - 2, own.shape[2]
    across = [
        remote(own.at[1 + r], prior.at[1 + r], xs.at[r], xr.at[r], {"segment": here.s + 1}) for r in range(rows)
    ]
    tail = last_part(here, own, low_cache, gain_low, conv_up, conv_low, out, across, *last[:2], last[2], prior, *last[3:])

    def begun():
        for fetch in fetches:
            fetch.start()
        next(tail)

    def fold():
        for fetch in fetches:
            fetch.wait()
        wqk[...] = (dot_t(wqkv[:, :ch], wqkv[:, ch : 2 * ch]) * (math.log2(math.e) / math.sqrt(ch))).astype(BF)
        wvo[...] = dot(wqkv[:, 2 * ch :], wproj[...]).astype(BF)

    drains = [first_part(here, latent, cache_mid, gain_mid, conv_mid, every, begun, fold, *first)]
    drains.append(attn_part(here, lambda: next(tail), gain_attn, wqk, wvo, every, own, across, *attn))
    next(tail, None)
    for drain in drains:
        drain()


def call(kernel, number, outs, scratch, *args, far=()):
    return pl.pallas_call(
        kernel,
        out_shape=outs,
        in_specs=[pl.BlockSpec(memory_space=pl.ANY if i in far else pltpu.VMEM) for i in range(len(args))],
        out_specs=pl.BlockSpec(memory_space=pltpu.VMEM),
        scratch_shapes=scratch,
        compiler_params=pltpu.CompilerParams(
            collective_id=number, has_side_effects=True, vmem_limit_bytes=59500000
        ),
    )(*args)


def body(
    latent, cache_mid, cache_low, gain_mid, gain_attn, gain_low, conv_mid, attn_qkv, attn_proj, conv_up, conv_low
):
    frames, rows, width, ch = latent.shape
    part = conv_mid.shape[-1]
    dma, one = pltpu.SemaphoreType.DMA, pltpu.SemaphoreType.DMA(())
    taps_t, taps_h, taps_w = conv_mid.shape[:3]
    total = rows * lax.axis_size("rows")
    cache_t = jnp.swapaxes(cache_low, 2, 3)
    tile = pltpu.VMEM((rows + 2, width, ch), BF)
    shared = [
        pltpu.VMEM((total, width, ch), BF), tile, tile,
        pltpu.VMEM(attn_qkv.shape, BF), pltpu.VMEM(attn_proj.shape, BF),
        pltpu.VMEM((ch, ch), BF), pltpu.VMEM((ch, ch), BF), pltpu.VMEM(cache_t.shape, BF),
        dma((3,)), dma((rows,)), dma((rows,)),
    ]
    first = [
        pltpu.VMEM(latent.shape, BF),
        pltpu.VMEM((taps_t - 1 + frames, rows, width, ch), BF),
        pltpu.VMEM((taps_t, taps_h, taps_w, part, ch), BF),
        pltpu.VMEM((taps_w, frames, rows + 2, width, part), F32),
        pltpu.VMEM((2, frames, width // 2, 2 * part), BF),
        pltpu.VMEM((2, frames, width // 2, 2 * part), BF),
        pltpu.VMEM((frames, rows, width, ch), BF),
        pltpu.VMEM((rows, width, ch), BF),
        dma((2, frames)), dma((2, frames)), *(dma((taps_t - 1,)) for _ in range(4)), one, one, dma((2,)), dma((taps_h,)),
    ]
    sizes = (rows * width, 2 * width)
    attn = [
        pltpu.VMEM((total, width, ch), BF),
        *(pltpu.VMEM((n, ch), BF) for n in sizes),
        *(pltpu.VMEM((n, ch), F32) for n in sizes),
        *(pltpu.VMEM((n, 1), F32) for n in sizes),
        *(pltpu.VMEM((n, 1), F32) for n in sizes),
        dma((total, 2)),
        dma((total,)),
    ]
    _, tall, wide, low = cache_low.shape
    cut = conv_low.shape[-1]
    two = 2 * low
    taps_t, taps_h, taps_w = conv_low.shape[:3]
    last = [
        pltpu.VMEM((2 * frames, 2 * (tall + 2), width, two), BF),
        pltpu.VMEM((frames * tall * width, 2 * cut), F32),
        pltpu.VMEM((taps_t, taps_h, taps_w * low, cut), BF),
        pltpu.VMEM((2, frames, low, wide), BF),
        pltpu.VMEM((2, 3, 3, cut, ch), BF),
        pltpu.VMEM((2, 2 * two, 2 * ch), BF),
        pltpu.VMEM((taps_t, taps_h, 2 * two, 2 * cut), BF),
        pltpu.VMEM((2, rows + 1, width, 2 * two), F32),
        pltpu.VMEM((frames, tall, width, two), BF),
        pltpu.VMEM((2, frames * tall, cut, width), BF),
        dma((2,)), dma((2,)), dma((2,)), dma((2,)), one, one, one, one,
        dma((2, tall + 2)), dma((2, tall + 2)), dma((tall,)), dma((tall,)),
    ]
    args = (
        latent, cache_mid, cache_t, gain_mid, gain_attn, gain_low, jnp.swapaxes(conv_mid, 3, 4), attn_qkv, attn_proj,
        jnp.swapaxes(conv_up, 2, 3), conv_low.reshape(taps_t, taps_h, taps_w * low, cut),
    )
    counts = (len(args), 1, len(shared), len(first), len(attn), len(last))
    decoded = call(
        functools.partial(whole_kernel, counts),
        0,
        pltpu.VMEM((frames, tall, cut, wide), BF),
        shared + first + attn + last,
        *args,
        far=(0, 1, 2, 6, 7, 8, 9, 10),
    )
    return jnp.swapaxes(decoded, 2, 3)


def solution(mesh):
    placed = (
        P(("groups", "segment"), "rows", None, None),
        P("groups", "rows", None, None),
        P("groups", "rows", None, None),
        P(),
        P(),
        P(),
        P(None, None, None, None, "chan"),
        P(),
        P(),
        P(None, None, None, "chan"),
        P(None, None, None, None, "chan"),
    )
    return jax.shard_map(
        body,
        mesh=mesh,
        in_specs=placed,
        out_specs=P(("groups", "segment"), "rows", None, "chan"),
        check_vma=False,
    )
```
